32 devices in a mesh: stick: 2 (over x), band: 16 (over z, y, core).
Axes of the slice: x: 2, y: 2, z: 4, core: 2. Of those that a mesh axis runs over, the one named last changes fastest.
Arguments:
- orbital_sticks: bfloat16 [32, 6144, 128], P('band', 'stick'), may hold values from -5 to 5
- stick_perm: int32 [4096], replicated, may hold values from 0 to 4095, each once
- stick_counts: int32 [2], replicated, may hold values from 1 to 3072, 4096 in all
- source_ids: int32 [1], replicated, may hold values from 0 to 31
Outputs:
- exchange: bfloat16 [32, 64, 64, 128], P(('band', 'stick'))
The draws below stay inside these ranges and needn't reach their ends.
All inputs are finite; a program needn't handle non-finite values.
Results may differ from the reference program's by a relative error of at most 0.001.
Values may be sent and summed in bfloat16 or wider, within the bound.
A program may use at most 64 MiB of HBM per device.

```python
import math
import jax
import jax.numpy as jnp
import numpy as np
from jax import lax

NX = 64
NY = 64
NZ = 128
NSRC = 1
NB = 32
NXY = 4096
CAP = 3072
SLOTS = 6144
N_STICK = 2


def block_scale(rng, extent, split, smallest, largest):
    factor_of, own = 1.0, jax.random.fold_in(rng, 6)
    for dim, blocks in split:
        steps = jnp.exp(jax.random.uniform(jax.random.fold_in(own, dim), (blocks,), jnp.float32, smallest / len(split), largest / len(split)))
        factor_of = factor_of * jnp.repeat(steps, extent[dim] // blocks).reshape([-1 if axis == dim else 1 for axis in range(len(extent))])
    return factor_of


def profile(amount, total, reach, slope):
    portions = [(1 << 20) // math.isqrt(rank ** slope) + 1 for rank in range(2, amount + 1)]
    spare, given = total - reach - (amount - 1), [1] * (amount - 1)
    while spare > 0:
        movable = [i for i in range(amount - 1) if given[i] < reach]
        pool, remaining = sum([portions[i] for i in movable]), spare
        for i in movable:
            extra = min(reach - given[i], max(1, remaining * portions[i] // pool), spare)
            given[i] = given[i] + extra
            spare = spare - extra
    return np.array([reach] + given)


def ragged(stream_key, number_of, total, bound, skew):
    if number_of == 2:
        one = jax.random.randint(stream_key, (), max(1, total - bound), min(bound, total - 1) + 1)
        return jnp.stack([one, total - one])
    tallies = jnp.asarray(profile(number_of, total, bound, skew), jnp.int32)
    twos = (number_of - 1) // 2
    source_of, sink = tallies[1:1 + 2 * twos:2], tallies[2:2 + 2 * twos:2]
    slack = jnp.minimum(source_of - 1, bound - sink)
    passed = jax.random.randint(jax.random.fold_in(stream_key, 1), (twos,), 0, 1 << 20) % (slack + 1)
    tallies = tallies.at[1:1 + 2 * twos:2].set(source_of - passed).at[2:2 + 2 * twos:2].set(sink + passed)
    return tallies[jax.random.permutation(jax.random.fold_in(stream_key, 2), number_of)]


def centred(key, shape, spread, reach, pieces=(), held_as=jnp.bfloat16):
    drawn = jax.random.normal(key, shape, jnp.float32) * spread
    if len(pieces) > 0:
        drawn = block_scale(key, shape, pieces, -0.22, 0.18) * drawn
    return jnp.clip(drawn, min=-reach, max=reach).astype(held_as)


def setup_inputs(seed: int = 0) -> dict:
    seeds = jax.random.split(jax.random.key(seed), 5)
    orbital_sticks = centred(seeds[0], (NB, SLOTS, NZ), 0.7, 5.0, ((0, 16), (1, 2)))
    stick_perm = jax.random.permutation(seeds[1], NXY).astype(jnp.int32)
    stick_counts = ragged(seeds[2], N_STICK, NXY, CAP, 2).astype(jnp.int32)
    source_ids = jax.random.randint(seeds[3], (NSRC,), 0, NB).astype(jnp.int32)
    return dict(orbital_sticks=orbital_sticks, stick_perm=stick_perm, stick_counts=stick_counts, source_ids=source_ids)


screen_omega = 0.25


def slot_targets(stick_perm, stick_counts):
    slots = jnp.arange(SLOTS, dtype=jnp.int32)
    holder = slots // CAP
    within = slots % CAP
    offsets = jnp.cumsum(stick_counts).astype(jnp.int32) - stick_counts
    valid = within < stick_counts[holder]
    position = jnp.clip(offsets[holder] + within, 0, NX * NY - 1).astype(jnp.int32)
    return jnp.where(valid, stick_perm[position], NX * NY).astype(jnp.int32)


def place_sticks(blocks, targets):
    empty = jnp.zeros((blocks.shape[0], NX * NY + 1, NZ), blocks.dtype)
    filled = empty.at[:, targets].set(blocks)
    return filled[:, :NX * NY].reshape(blocks.shape[0], NX, NY, NZ)


def signed_freq(length):
    steps = jnp.arange(length, dtype=jnp.int32)
    signed = jnp.where(steps <= length // 2, steps, steps - length)
    return signed.astype(jnp.float32) / length


def screened(freq_x, freq_y, freq_z):
    square = (2.0 * math.pi) ** 2 * (freq_x[:, None, None] ** 2 + freq_y[None, :, None] ** 2 + freq_z[None, None, :] ** 2)
    safe = jnp.where(square > 0, square, 1.0)
    inner = 4.0 * math.pi * (1.0 - jnp.exp(-square / (4.0 * screen_omega ** 2))) / safe
    return jnp.where(square > 0, inner, math.pi / screen_omega ** 2)


def reference(orbital_sticks, stick_perm, stick_counts, source_ids):
    targets = slot_targets(stick_perm, stick_counts)
    half_z = jnp.arange(NZ // 2 + 1, dtype=jnp.int32).astype(jnp.float32) / NZ
    kernel = screened(signed_freq(NX), signed_freq(NY), half_z)
    sources = place_sticks(orbital_sticks[source_ids], targets).astype(jnp.float32)

    def one_band(band):
        block = lax.dynamic_slice_in_dim(orbital_sticks, band, 1, 0)
        orbital = place_sticks(block, targets)[0].astype(jnp.float32)
        total = jnp.zeros((NX, NY, NZ), jnp.float32)
        for which in range(NSRC):
            density = orbital * sources[which]
            potential = jnp.fft.irfftn(jnp.fft.rfftn(density) * kernel, s=(NX, NY, NZ))
            total = total + sources[which] * potential
        return (-total).astype(jnp.bfloat16)

    return lax.map(one_band, jnp.arange(NB, dtype=jnp.int32))
```

```python
import functools
import math

import jax
import jax.numpy as jnp
import numpy as np
from jax import lax
from jax.experimental import pallas as pl
from jax.experimental.pallas import tpu as pltpu
from jax.sharding import PartitionSpec as P

NX = 64
NY = 64
NZ = 128
CHUNKS = 8
LAG = 3
UNIT = 64
SPAN = 256
LINES = 16
ROWS = 512
ROOT = math.sqrt(2.0)
HALF = math.sqrt(0.5)

screen_omega = 0.25


def signed_freq(length):
    steps = np.arange(length, dtype=np.int32)
    signed = np.where(steps <= length // 2, steps, steps - length)
    return signed.astype(np.float64) / length


def screened(freq_x, freq_y, freq_z):
    square = (2.0 * math.pi) ** 2 * (
        freq_x[:, None, None] ** 2 + freq_y[None, :, None] ** 2 + freq_z[None, None, :] ** 2
    )
    safe = np.where(square > 0, square, 1.0)
    inner = 4.0 * math.pi * (1.0 - np.exp(-square / (4.0 * screen_omega**2))) / safe
    return np.where(square > 0, inner, math.pi / screen_omega**2)


def hartley_table(length):
    steps = np.arange(length, dtype=np.int64)
    angle = (steps[:, None] * steps[None, :] % length) * (2.0 * math.pi / length)
    return np.cos(angle) + np.sin(angle)


def halves(table):
    high = table.astype(jnp.bfloat16)
    low = (table - high.astype(np.float64)).astype(jnp.bfloat16)
    return high, low


def band_shape(bands):
    return (bands // 4, 2, 2) if bands % 4 == 0 else (bands, 1, 1)


def spread_kernel(root, sticks, shape, chunk, piece, mine, source, owned, tree_send, tree_recv,
                  peer_send, peer_recv, core_send, core_recv, swap_send, swap_recv):
    lines, wide, cores = shape
    stick = lax.axis_index("stick")
    band = lax.axis_index("band")
    core = band % cores
    row = (band // cores) % wide
    line = band // (cores * wide)
    root_core = root % cores
    root_row = (root // cores) % wide
    root_line = root // (cores * wide)
    place = lambda l, r, c: (l * wide + r) * cores + c

    barrier = pltpu.get_barrier_semaphore()

    def greet(**where):
        pl.semaphore_signal(barrier, inc=1, device_id=where, device_id_type=pl.DeviceIdType.MESH)

    pl.when(line > 0)(lambda: greet(band=place(line - 1, row, core)))
    pl.when(line < lines - 1)(lambda: greet(band=place(line + 1, row, core)))
    for step in range(1, wide):
        greet(band=place(line, (row + step) % wide, core))
    for step in range(1, cores):
        greet(band=place(line, row, (core + step) % cores))
    for step in range(1, sticks):
        greet(stick=(stick + step) % sticks)
    near = jnp.where(line > 0, 1, 0) + jnp.where(line < lines - 1, 1, 0)
    pl.semaphore_wait(barrier, near + (wide - 1) + (cores - 1) + (sticks - 1))

    def remote(src, dst, send, recv, **where):
        return pltpu.make_async_remote_copy(
            src_ref=src, dst_ref=dst, send_sem=send, recv_sem=recv,
            device_id=where, device_id_type=pl.DeviceIdType.MESH)

    def swap(step, k):
        rows = pl.ds(pl.multiple_of(k * chunk, chunk), chunk)
        peer = (stick + step) % sticks
        return remote(mine.at[peer, rows], owned.at[stick, rows], swap_send.at[step, k], swap_recv.at[step, k],
                      stick=peer)

    primary = core == root_core
    is_root = band == root

    def tree(slot, k, target):
        rows = pl.ds(pl.multiple_of(k * chunk, chunk), chunk)
        return lambda src: remote(src.at[rows], source.at[stick, rows], tree_send.at[slot, k], tree_recv.at[k],
                                  band=target)

    up_ok = primary & (row == root_row) & (line >= root_line) & (line < lines - 1)
    down_ok = primary & (row == root_row) & (line <= root_line) & (line > 0)
    side_ok = primary & (row == root_row)
    exits = [(up_ok, place(line + 1, row, core)), (down_ok, place(line - 1, row, core))]
    exits += [(side_ok, place(line, (row + step) % wide, core)) for step in range(1, wide)]

    def fan(k, src):
        rows = pl.ds(pl.multiple_of(k * chunk, chunk), chunk)
        for slot, (allowed, target) in enumerate(exits):
            pl.when(allowed)(lambda slot=slot, target=target: tree(slot, k, target)(src).start())
        for step in range(1, sticks):
            remote(src.at[rows], source.at[stick, rows], peer_send.at[step, k], peer_recv.at[step, k],
                   stick=(stick + step) % sticks).start()
        for step in range(1, cores):
            remote(src.at[rows], source.at[stick, rows], core_send.at[step, 0, k], core_recv.at[0, k],
                   band=place(line, row, (core + step) % cores)).start()

    def tree_arrival(k):
        rows = pl.ds(pl.multiple_of(k * chunk, chunk), chunk)
        return remote(source.at[stick, rows], source.at[stick, rows], tree_send.at[0, k], tree_recv.at[k],
                      band=place(line, (row + 1) % wide, core))

    def peer_copy(step, k):
        rows = pl.ds(pl.multiple_of(k * chunk, chunk), chunk)
        peer = (stick + step) % sticks
        return peer, remote(source.at[stick, rows], source.at[stick, rows], peer_send.at[step, k],
                            peer_recv.at[step, k], stick=peer)

    def relay(k):
        rows = pl.ds(pl.multiple_of(k * chunk, chunk), chunk)
        for step in range(1, sticks):
            peer_copy(step, k)[1].wait_recv()
            sender = (stick + sticks - step) % sticks
            for other in range(1, cores):
                remote(source.at[sender, rows], source.at[sender, rows], core_send.at[other, step, k],
                       core_recv.at[step, k], band=place(line, row, (core + other) % cores)).start()

    @pl.when(primary)
    def _():
        @pl.loop(0, CHUNKS)
        def _(k):
            @pl.when(is_root)
            def _():
                fan(k, piece)

            @pl.when(jnp.logical_not(is_root))
            def _():
                tree_arrival(k).wait_recv()
                fan(k, source.at[stick])

            for step in range(1, sticks):
                swap(step, k).start()
            pl.when(k >= LAG)(lambda: relay(k - LAG))

        @pl.loop(CHUNKS - LAG, CHUNKS)
        def _(k):
            relay(k)

    @pl.when(jnp.logical_not(primary))
    def _():
        @pl.loop(0, CHUNKS)
        def _(k):
            for step in range(1, sticks):
                swap(step, k).start()

        @pl.loop(0, CHUNKS)
        def _(k):
            rows = pl.ds(pl.multiple_of(k * chunk, chunk), chunk)
            for step in range(sticks):
                sender = (stick + sticks - step) % sticks
                remote(source.at[sender, rows], source.at[sender, rows], core_send.at[0, step, k],
                       core_recv.at[step, k], band=place(line, row, (core + 1) % cores)).wait_recv()

    @pl.when(primary)
    def _():
        @pl.loop(0, CHUNKS)
        def _(k):
            for slot, (allowed, target) in enumerate(exits):
                pl.when(allowed)(lambda slot=slot, target=target: tree(slot, k, target)(piece).wait_send())
            for step in range(1, sticks):
                peer_copy(step, k)[1].wait_send()
            rows = pl.ds(pl.multiple_of(k * chunk, chunk), chunk)
            for other in range(1, cores):
                for step in range(sticks):
                    sender = (stick + sticks - step) % sticks
                    remote(source.at[sender, rows], source.at[sender, rows], core_send.at[other, step, k],
                           core_recv.at[step, k], band=place(line, row, (core + other) % cores)).wait_send()

    @pl.loop(0, CHUNKS)
    def _(k):
        for step in range(1, sticks):
            swap(step, k).wait()


def spread(root, sticks, bands, piece, mine):
    capacity, depth = piece.shape
    shape = band_shape(bands)
    lines, wide, cores = shape
    dma = pltpu.SemaphoreType.DMA
    block = jax.ShapeDtypeStruct((sticks, capacity, depth), piece.dtype)
    anywhere = pl.BlockSpec(memory_space=pl.ANY)
    return pl.pallas_call(
        functools.partial(spread_kernel, root, sticks, shape, capacity // CHUNKS),
        out_shape=(block, block),
        in_specs=[anywhere, anywhere],
        out_specs=(anywhere, anywhere),
        scratch_shapes=[
            dma((wide + 1, CHUNKS)),
            dma((CHUNKS,)),
            dma((sticks, CHUNKS)),
            dma((sticks, CHUNKS)),
            dma((cores, sticks, CHUNKS)),
            dma((sticks, CHUNKS)),
            dma((sticks, CHUNKS)),
            dma((sticks, CHUNKS)),
        ],
        compiler_params=pltpu.CompilerParams(collective_id=root, has_side_effects=True),
    )(piece, mine)


def spread_far(group, piece, mine):
    is_root = lax.axis_index("band") == group
    piece = lax.psum(jnp.where(is_root, piece, jnp.zeros_like(piece)), "band")
    source = lax.all_gather(piece, "stick", axis=0, tiled=False)
    owned = lax.all_to_all(mine, "stick", split_axis=0, concat_axis=0, tiled=True)
    return source, owned


def split(value):
    high = value.astype(jnp.bfloat16)
    low = (value - high.astype(jnp.float32)).astype(jnp.bfloat16)
    return high, low


def left(table, value):
    high, low = split(value)
    return jnp.dot(table, jnp.concatenate([high, low, high], axis=0), preferred_element_type=jnp.float32)


def along_z(value, table):
    high, low = split(value)
    both = jnp.dot(jnp.concatenate([high, low], axis=1), table, preferred_element_type=jnp.float32)
    return both[:, :NZ] + both[:, NZ:]


def hartley8(x):
    s = [x[i] + x[i + 4] for i in range(4)]
    d = [x[i] - x[i + 4] for i in range(4)]
    p, q, r, u = s[0] + s[2], s[1] + s[3], s[0] - s[2], s[1] - s[3]
    e, f, g, h = d[0] + d[2], d[0] - d[2], d[1] * ROOT, d[3] * ROOT
    return [p + q, e + g, r + u, f + h, p - q, e - g, r - u, f - h]


def plus(a, b):
    return a[0] + b[0], a[1] + b[1]


def minus(a, b):
    return a[0] - b[0], a[1] - b[1]


def fourier4(x, sign):
    a, b, c, d = plus(x[0], x[2]), minus(x[0], x[2]), plus(x[1], x[3]), minus(x[1], x[3])
    ahead, back = (b[0] - d[1], b[1] + d[0]), (b[0] + d[1], b[1] - d[0])
    if sign < 0:
        ahead, back = back, ahead
    return [plus(a, c), ahead, minus(a, c), back]


def fourier8(x, sign):
    even = fourier4([plus(x[i], x[i + 4]) for i in range(4)], sign)
    d = [minus(x[i], x[i + 4]) for i in range(4)]
    (a, b), (p, q), (u, v) = d[1], d[2], d[3]
    if sign > 0:
        turned = [((a - b) * HALF, (a + b) * HALF), (-q, p), ((u + v) * -HALF, (u - v) * HALF)]
    else:
        turned = [((a + b) * HALF, (b - a) * HALF), (q, -p), ((v - u) * HALF, (u + v) * -HALF)]
    odd = fourier4([d[0]] + turned, sign)
    return [value for both in zip(even, odd) for value in both]


def rotate(value, step, sign):
    if step == 0:
        return value
    c, s = math.cos(2 * math.pi * step / NX), sign * math.sin(2 * math.pi * step / NX)
    return value[0] * c - value[1] * s, value[1] * c + value[0] * s


def combine(get, put):
    for k, value in enumerate(hartley8([get(b, 0) for b in range(8)])):
        put(8 * k, value)
    for first in range(1, 4):
        mixed = fourier8([rotate((get(b, first), get(b, 8 - first)), b * first, -1) for b in range(8)], -1)
        for k, (p, q) in enumerate(mixed):
            put(first + 8 * k, p)
            put(NX - first - 8 * k, q)
    mixed = fourier8([rotate((get(b, 4), jnp.zeros_like(get(b, 4))), b * 4, -1) for b in range(8)], -1)
    for k in range(4):
        put(4 + 8 * k, mixed[k][0] - mixed[k][1])
        put(NX - 4 - 8 * k, mixed[k][0] + mixed[k][1])


def separate(get, put):
    for b, value in enumerate(hartley8([get(8 * k) for k in range(8)])):
        put(b, 0, value)
    for first in range(1, 4):
        mixed = fourier8([(get(first + 8 * k), get(NX - first - 8 * k)) for k in range(8)], 1)
        for b in range(8):
            p, q = rotate(mixed[b], b * first, 1)
            put(b, first, p)
            put(b, 8 - first, q)
    mixed = fourier8([(get(4 + 8 * k), jnp.zeros_like(get(4))) for k in range(8)], 1)
    for b in range(8):
        p, q = rotate(mixed[b], b * 4, 1)
        put(b, 4, p + q)


def exchange_kernel(sticks, capacity, target, counts, facts, owned_far, source_far, mine, table_y, table_z,
                    kernel, out, owned, source, sem, slot, grid, turned, work):
    stick, is_root, root_row = facts[0], facts[1], facts[2]
    unit = math.gcd(capacity, UNIT)
    span = math.gcd(capacity, SPAN)

    def fetch(block):
        at = pl.ds(block * capacity, capacity)
        bring = lambda src, dst, which: pltpu.make_async_copy(src, dst.at[at], sem.at[which, block]).start()
        here = block == stick
        pl.when(here)(lambda: bring(mine.at[block], owned, 0))
        pl.when(jnp.logical_not(here))(lambda: bring(owned_far.at[block], owned, 0))
        from_mine = here & (is_root == 1)
        pl.when(from_mine)(lambda: bring(mine.at[root_row], source, 1))
        pl.when(jnp.logical_not(from_mine))(lambda: bring(source_far.at[block], source, 1))

    for block in range(sticks):
        fetch(block)

    offset = 0
    for block in range(sticks):
        count = counts[block]
        base = block * capacity
        at_block = pl.ds(base, capacity)
        pltpu.make_async_copy(owned_far.at[block], owned.at[at_block], sem.at[0, block]).wait()
        pltpu.make_async_copy(source_far.at[block], source.at[at_block], sem.at[1, block]).wait()

        @pl.loop(0, pl.cdiv(count, span))
        def _(i):
            first = pl.multiple_of(base + i * span, span)
            value = source[pl.ds(first, span), :].astype(jnp.float32)
            slot[pl.ds(2 * first, span, stride=2), :] = owned[pl.ds(first, span), :].astype(jnp.float32) * value
            slot[pl.ds(2 * first + 1, span, stride=2), :] = value

        @pl.loop(0, pl.cdiv(count, unit))
        def _(j):
            for u in range(unit):
                i = j * unit + u
                grid[pl.ds(target[offset + i], 2), :] = slot[pl.ds(2 * (base + i), 2), :]

        offset = offset + count

    plane = lambda x: pl.ds(x * NY, NY)
    within = lambda x, which: pl.ds(2 * NY * x + which, NY, stride=2)

    for b in range(8):
        value = []
        for a in range(0, 8, 2):
            both = jnp.concatenate([grid[within(8 * (a + i) + b, 0), :] for i in range(2)], axis=1)
            both = left(table_y[...], both)
            value += [both[:, :NZ], both[:, NZ:]]
        for k, part in enumerate(hartley8(value)):
            turned[plane(8 * b + k), :] = part

    def part_of(j):
        return lambda x: pl.ds(pl.multiple_of(x * NY + j * LINES, LINES), LINES)

    @pl.loop(0, NY // LINES)
    def _(j):
        at = part_of(j)
        combine(lambda b, k: turned[at(8 * b + k), :], lambda x, v: work.__setitem__((at(x), slice(None)), v))

    for i in range(NX * NY // ROWS):
        at = pl.ds(i * ROWS, ROWS)
        work[at, :] = along_z(along_z(work[at, :], table_z[...]) * kernel[at, :], table_z[...])

    @pl.loop(0, NY // LINES)
    def _(j):
        at = part_of(j)
        separate(lambda x: work[at(x), :], lambda b, k, v: turned.__setitem__((at(8 * b + k), slice(None)), v))

    for b in range(8):
        value = hartley8([turned[plane(8 * b + k), :] for k in range(8)])
        for a in range(0, 8, 2):
            both = left(table_y[...], jnp.concatenate(value[a:a + 2], axis=1))
            for i in range(2):
                x = 8 * (a + i) + b
                part = both[:, i * NZ:(i + 1) * NZ]
                out[plane(x), :] = (part * grid[within(x, 1), :]).astype(jnp.bfloat16)


def exchange(stick_perm, stick_counts, facts, owned, source, mine):
    sticks, capacity, depth = owned.shape
    table_y, low_y = halves(hartley_table(NY))
    table_z, low_z = halves(hartley_table(NZ))
    left_y = jnp.asarray(np.concatenate([table_y, table_y, low_y], axis=1))
    right_z = np.concatenate(
        [np.concatenate([table_z, low_z], axis=1), np.concatenate([table_z, np.zeros_like(low_z)], axis=1)], axis=0)
    right_z = jnp.asarray(right_z)
    kernel = screened(signed_freq(NX), signed_freq(NY), signed_freq(NZ)) * (-1.0 / (NX * NY * NZ))
    kernel = jnp.asarray(kernel.reshape(NX * NY, NZ), jnp.float32)
    target = jnp.pad(stick_perm * 2, (0, UNIT), constant_values=2 * NX * NY)
    smem = pl.BlockSpec(memory_space=pltpu.SMEM)
    vmem = pl.BlockSpec(memory_space=pltpu.VMEM)
    anywhere = pl.BlockSpec(memory_space=pl.ANY)
    slots = sticks * capacity
    full = lambda n: pltpu.VMEM((n, NZ), jnp.float32)
    return pl.pallas_call(
        functools.partial(exchange_kernel, sticks, capacity),
        out_shape=jax.ShapeDtypeStruct((NX * NY, NZ), jnp.bfloat16),
        in_specs=[smem] * 3 + [anywhere] * 3 + [vmem] * 3,
        out_specs=vmem,
        scratch_shapes=[pltpu.VMEM((slots, NZ), jnp.bfloat16), pltpu.VMEM((slots, NZ), jnp.bfloat16),
                        pltpu.SemaphoreType.DMA((2, sticks)), full(2 * slots), full(2 * NX * NY + 8), full(NX * NY),
                        full(NX * NY)],
        compiler_params=pltpu.CompilerParams(vmem_limit_bytes=40 << 20),
    )(target, stick_counts, facts, owned, source, mine, left_y, right_z, kernel)


def local(orbital_sticks, stick_perm, stick_counts, source_ids):
    sticks = lax.axis_size("stick")
    bands = lax.axis_size("band")
    rows = orbital_sticks.shape[0]
    group = source_ids[0] // rows
    piece = lax.dynamic_index_in_dim(orbital_sticks, source_ids[0] % rows, 0, keepdims=False)
    if bands <= 16:
        branches = [functools.partial(spread, root, sticks, bands) for root in range(bands)]
        source, owned = lax.switch(group, branches, piece, orbital_sticks)
    else:
        source, owned = spread_far(group, piece, orbital_sticks)
    row = source_ids[0] % rows
    is_root = (lax.axis_index("band") == group).astype(jnp.int32)
    facts = jnp.stack([lax.axis_index("stick"), is_root, row]).astype(jnp.int32)
    out = exchange(stick_perm, stick_counts, facts, owned, source, orbital_sticks)
    return out.reshape(1, NX, NY, NZ)


def solution(mesh):
    placed = (P("band", "stick", None), P(), P(), P())
    return jax.shard_map(
        local,
        mesh=mesh,
        in_specs=placed,
        out_specs=P(("band", "stick"), None, None, None),
        check_vma=False,
    )
```

```python
import functools
import math

import jax
import jax.numpy as jnp
import numpy as np
from jax import lax
from jax.experimental import pallas as pl
from jax.experimental.pallas import tpu as pltpu
from jax.sharding import PartitionSpec as P

NX = 64
NY = 64
NZ = 128
EACH = 8
WIDE = 2
CORES = 2
PARTS = 8
SECOND_EARLY = 2
BESIDE_EARLY = 2
LAG = 8
UNIT = 64
SPAN = 256
LINES = 16
ROWS = 512
ROOT = math.sqrt(2.0)
HALF = math.sqrt(0.5)

screen_omega = 0.25


def signed_freq(length):
    steps = np.arange(length, dtype=np.int32)
    signed = np.where(steps <= length // 2, steps, steps - length)
    return signed.astype(np.float64) / length


def screened(freq_x, freq_y, freq_z):
    square = (2.0 * math.pi) ** 2 * (
        freq_x[:, None, None] ** 2 + freq_y[None, :, None] ** 2 + freq_z[None, None, :] ** 2
    )
    safe = np.where(square > 0, square, 1.0)
    inner = 4.0 * math.pi * (1.0 - np.exp(-square / (4.0 * screen_omega**2))) / safe
    return np.where(square > 0, inner, math.pi / screen_omega**2)


def hartley_table(length):
    steps = np.arange(length, dtype=np.int64)
    angle = (steps[:, None] * steps[None, :] % length) * (2.0 * math.pi / length)
    return np.cos(angle) + np.sin(angle)


def halves(table):
    high = table.astype(jnp.bfloat16)
    low = (table - high.astype(np.float64)).astype(jnp.bfloat16)
    return high, low


def tree_of(lines, root):
    middle = 2 if root == 0 else lines - 3 if root == lines - 1 else -1
    if lines == 4 and middle >= 0:
        return {root: [middle], middle: [middle - 1, middle + 1]} if root == 0 else {root: [middle], middle: [middle + 1, middle - 1]}
    tree = {}
    for line in range(lines):
        if line < root:
            tree.setdefault(line + 1, []).append(line)
        if line > root:
            tree.setdefault(line - 1, []).append(line)
    return tree


def spread_kernel(root, lines, row, mine, source, owned, stage, piece, stage_sem, send, arrived, swap_send, swap_recv):
    rows, capacity, _ = mine.shape
    chunk = capacity // (2 * EACH)
    stick = lax.axis_index("stick")
    band = lax.axis_index("band")
    core = band % CORES
    side = (band // CORES) % WIDE
    line = band // (CORES * WIDE)
    root_core = root % CORES
    root_side = (root // CORES) % WIDE
    root_line = root // (CORES * WIDE)
    place = lambda l, r, c: (l * WIDE + r) * CORES + c
    tree = tree_of(lines, root_line)
    is_root = band == root
    half = (core + root_core) % 2
    here = line == root_line
    near = (side + root_side) % 2 == half
    origin = here & near
    second = origin & (half == 1)

    fetch = [pltpu.make_async_copy(mine.at[r], stage.at[r], stage_sem.at[r]) for r in range(rows)]

    @pl.when(is_root)
    def _():
        for r in range(rows):
            fetch[r].start()

    barrier = pltpu.get_barrier_semaphore()

    def greet(**where):
        pl.semaphore_signal(barrier, inc=1, device_id=where, device_id_type=pl.DeviceIdType.MESH)

    hops = [(parent, child) for parent in sorted(tree) for child in tree[parent]]
    count = 3
    for parent, child in hops:
        pl.when(near & (line == parent))(lambda child=child: greet(band=place(child, side, core)))
        pl.when(near & (line == child))(lambda parent=parent: greet(band=place(parent, side, core)))
        count = count + jnp.where(near & (line == parent), 1, 0) + jnp.where(near & (line == child), 1, 0)
    greet(band=place(line, 1 - side, core))
    greet(band=place(line, side, 1 - core))
    greet(stick=1 - stick)
    pl.when(is_root)(lambda: greet(band=place(root_line, 1 - root_side, 1 - root_core)))
    pl.when(second)(lambda: greet(band=root))
    count = count + jnp.where(is_root, 1, 0) + jnp.where(second, 1, 0)

    @pl.when(is_root)
    def _():
        for r in range(rows):
            fetch[r].wait()

        @pl.loop(0, 2 * EACH)
        def _(q):
            at = pl.ds(pl.multiple_of(q * chunk, chunk), chunk)
            value = stage[0, at, :]
            for r in range(1, rows):
                value = jnp.where(row[0] == r, stage[r, at, :], value)
            piece[at, :] = value

    pl.semaphore_wait(barrier, count)

    def remote(src, dst, sent, came, where):
        return pltpu.make_async_remote_copy(src_ref=src, dst_ref=dst, send_sem=sent, recv_sem=came, device_id=where,
                                            device_id_type=pl.DeviceIdType.MESH)

    def swap(part):
        at = pl.ds(pl.multiple_of(part * (capacity // PARTS), capacity // PARTS), capacity // PARTS)
        return remote(mine.at[1 - stick, at], owned.at[stick, at], swap_send.at[part], swap_recv.at[part],
                      dict(stick=1 - stick))

    def copy(slot, block, q, src, **where):
        at = pl.ds(pl.multiple_of(q * chunk, chunk), chunk)
        return remote(src.at[at], source.at[block, at], send.at[slot, block, q], arrived.at[block, q], where)

    beside = place(line, side, 1 - core)
    fan = max(len(children) for children in tree.values())
    to_root = here & (side == root_side) & (half == 1)
    early = lambda part: jnp.logical_not(here) | (second & (part < SECOND_EARLY)) | (here & jnp.logical_not(origin) & (part < BESIDE_EARLY))

    def exits(block, q, src, own, act):
        if own:
            pl.when(origin)(lambda: act(copy(fan + 2, block, q, src, stick=1 - stick)))
        for parent, children in tree.items():
            for n, child in enumerate(children):
                pl.when(near & (line == parent))(
                    lambda n=n, child=child: act(copy(n, block, q, src, band=place(child, side, core))))
        pl.when(near)(lambda: act(copy(fan, block, q, src, band=place(line, 1 - side, core))))
        send_beside = lambda: act(copy(fan + 1, block, q, src, band=beside))
        if own:
            pl.when(jnp.logical_not(to_root))(send_beside)
        else:
            send_beside()

    def to_second(q, act):
        act(copy(fan + 3, stick, q, piece, band=place(root_line, 1 - root_side, 1 - root_core)))

    def arrive(block, q):
        copy(fan + 1, block, q, source.at[block], band=beside).wait_recv()

    start = lambda job: job.start()
    finish = lambda job: job.wait_send()
    first = half * EACH
    ours, theirs = source.at[stick], source.at[1 - stick]

    @pl.loop(0, PARTS)
    def _(part):
        pl.when(early(part))(lambda: swap(part).start())

    def own_step(i):
        @pl.when(is_root)
        def _():
            to_second(EACH + i, start)
            exits(stick, i, piece, True, start)

        @pl.when(jnp.logical_not(is_root))
        def _():
            arrive(stick, first + i)
            exits(stick, first + i, ours, True, start)

    def other_step(i):
        arrive(1 - stick, first + i)
        exits(1 - stick, first + i, theirs, False, start)

    @pl.loop(0, LAG)
    def _(i):
        own_step(i)

    if LAG < EACH:
        @pl.loop(LAG, EACH)
        def _(i):
            own_step(i)
            other_step(i - LAG)

    @pl.loop(0, PARTS)
    def _(part):
        pl.when(jnp.logical_not(early(part)))(lambda: swap(part).start())

    @pl.loop(EACH - LAG, EACH)
    def _(i):
        other_step(i)

    @pl.loop(0, EACH)
    def _(i):
        q = (1 - half) * EACH + i
        pl.when(jnp.logical_not(is_root))(lambda: arrive(stick, q))
        arrive(1 - stick, q)

    @pl.loop(0, EACH)
    def _(i):
        exits(stick, first + i, ours, True, finish)
        exits(1 - stick, first + i, theirs, False, finish)
        pl.when(is_root)(lambda: to_second(EACH + i, finish))

    @pl.loop(0, PARTS)
    def _(part):
        swap(part).wait()


def spread(root, lines, row, mine):
    rows, capacity, depth = mine.shape
    dma = pltpu.SemaphoreType.DMA
    block = jax.ShapeDtypeStruct((2, capacity, depth), mine.dtype)
    anywhere = pl.BlockSpec(memory_space=pl.ANY)
    return pl.pallas_call(
        functools.partial(spread_kernel, root, lines),
        out_shape=(block, block),
        in_specs=[pl.BlockSpec(memory_space=pltpu.SMEM), anywhere],
        out_specs=(anywhere, anywhere),
        scratch_shapes=[pltpu.VMEM((rows, capacity, depth), mine.dtype), pltpu.VMEM((capacity, depth), mine.dtype),
                        dma((rows,)), dma((6, 2, 2 * EACH)), dma((2, 2 * EACH)), dma((PARTS,)), dma((PARTS,))],
        compiler_params=pltpu.CompilerParams(collective_id=root, has_side_effects=True, vmem_limit_bytes=16 << 20),
    )(row, mine)


def spread_far(group, piece, mine):
    is_root = lax.axis_index("band") == group
    piece = lax.psum(jnp.where(is_root, piece, jnp.zeros_like(piece)), "band")
    source = lax.all_gather(piece, "stick", axis=0, tiled=False)
    owned = lax.all_to_all(mine, "stick", split_axis=0, concat_axis=0, tiled=True)
    return source, owned


def split(value):
    high = value.astype(jnp.bfloat16)
    low = (value - high.astype(jnp.float32)).astype(jnp.bfloat16)
    return high, low


def left(table, value):
    high, low = split(value)
    return jnp.dot(table, jnp.concatenate([high, low, high], axis=0), preferred_element_type=jnp.float32)


def along_z(value, table):
    high, low = split(value)
    both = jnp.dot(jnp.concatenate([high, low], axis=1), table, preferred_element_type=jnp.float32)
    return both[:, :NZ] + both[:, NZ:]


def hartley8(x):
    s = [x[i] + x[i + 4] for i in range(4)]
    d = [x[i] - x[i + 4] for i in range(4)]
    p, q, r, u = s[0] + s[2], s[1] + s[3], s[0] - s[2], s[1] - s[3]
    e, f, g, h = d[0] + d[2], d[0] - d[2], d[1] * ROOT, d[3] * ROOT
    return [p + q, e + g, r + u, f + h, p - q, e - g, r - u, f - h]


def plus(a, b):
    return a[0] + b[0], a[1] + b[1]


def minus(a, b):
    return a[0] - b[0], a[1] - b[1]


def fourier4(x, sign):
    a, b, c, d = plus(x[0], x[2]), minus(x[0], x[2]), plus(x[1], x[3]), minus(x[1], x[3])
    ahead, back = (b[0] - d[1], b[1] + d[0]), (b[0] + d[1], b[1] - d[0])
    if sign < 0:
        ahead, back = back, ahead
    return [plus(a, c), ahead, minus(a, c), back]


def fourier8(x, sign):
    even = fourier4([plus(x[i], x[i + 4]) for i in range(4)], sign)
    d = [minus(x[i], x[i + 4]) for i in range(4)]
    (a, b), (p, q), (u, v) = d[1], d[2], d[3]
    if sign > 0:
        turned = [((a - b) * HALF, (a + b) * HALF), (-q, p), ((u + v) * -HALF, (u - v) * HALF)]
    else:
        turned = [((a + b) * HALF, (b - a) * HALF), (q, -p), ((v - u) * HALF, (u + v) * -HALF)]
    odd = fourier4([d[0]] + turned, sign)
    return [value for both in zip(even, odd) for value in both]


def rotate(value, step, sign):
    if step == 0:
        return value
    c, s = math.cos(2 * math.pi * step / NX), sign * math.sin(2 * math.pi * step / NX)
    return value[0] * c - value[1] * s, value[1] * c + value[0] * s


def combine(get, put):
    for k, value in enumerate(hartley8([get(b, 0) for b in range(8)])):
        put(8 * k, value)
    for first in range(1, 4):
        mixed = fourier8([rotate((get(b, first), get(b, 8 - first)), b * first, -1) for b in range(8)], -1)
        for k, (p, q) in enumerate(mixed):
            put(first + 8 * k, p)
            put(NX - first - 8 * k, q)
    mixed = fourier8([rotate((get(b, 4), jnp.zeros_like(get(b, 4))), b * 4, -1) for b in range(8)], -1)
    for k in range(4):
        put(4 + 8 * k, mixed[k][0] - mixed[k][1])
        put(NX - 4 - 8 * k, mixed[k][0] + mixed[k][1])


def separate(get, put):
    for b, value in enumerate(hartley8([get(8 * k) for k in range(8)])):
        put(b, 0, value)
    for first in range(1, 4):
        mixed = fourier8([(get(first + 8 * k), get(NX - first - 8 * k)) for k in range(8)], 1)
        for b in range(8):
            p, q = rotate(mixed[b], b * first, 1)
            put(b, first, p)
            put(b, 8 - first, q)
    mixed = fourier8([(get(4 + 8 * k), jnp.zeros_like(get(4))) for k in range(8)], 1)
    for b in range(8):
        p, q = rotate(mixed[b], b * 4, 1)
        put(b, 4, p + q)


def exchange_kernel(sticks, capacity, target, counts, facts, owned_far, source_far, mine, table_y, table_z,
                    kernel, out, owned, source, sem, slot, grid, turned, work):
    stick, is_root, root_row = facts[0], facts[1], facts[2]
    unit = math.gcd(capacity, UNIT)
    span = math.gcd(capacity, SPAN)

    def fetch(block):
        at = pl.ds(block * capacity, capacity)
        bring = lambda src, dst, which: pltpu.make_async_copy(src, dst.at[at], sem.at[which, block]).start()
        here = block == stick
        pl.when(here)(lambda: bring(mine.at[block], owned, 0))
        pl.when(jnp.logical_not(here))(lambda: bring(owned_far.at[block], owned, 0))
        from_mine = here & (is_root == 1)
        pl.when(from_mine)(lambda: bring(mine.at[root_row], source, 1))
        pl.when(jnp.logical_not(from_mine))(lambda: bring(source_far.at[block], source, 1))

    for block in range(sticks):
        fetch(block)

    offset = 0
    for block in range(sticks):
        count = counts[block]
        base = block * capacity
        at_block = pl.ds(base, capacity)
        pltpu.make_async_copy(owned_far.at[block], owned.at[at_block], sem.at[0, block]).wait()
        pltpu.make_async_copy(source_far.at[block], source.at[at_block], sem.at[1, block]).wait()

        @pl.loop(0, pl.cdiv(count, span))
        def _(i):
            first = pl.multiple_of(base + i * span, span)
            value = source[pl.ds(first, span), :].astype(jnp.float32)
            slot[pl.ds(2 * first, span, stride=2), :] = owned[pl.ds(first, span), :].astype(jnp.float32) * value
            slot[pl.ds(2 * first + 1, span, stride=2), :] = value

        @pl.loop(0, pl.cdiv(count, unit))
        def _(j):
            for u in range(unit):
                i = j * unit + u
                grid[pl.ds(target[offset + i], 2), :] = slot[pl.ds(2 * (base + i), 2), :]

        offset = offset + count

    plane = lambda x: pl.ds(x * NY, NY)
    within = lambda x, which: pl.ds(2 * NY * x + which, NY, stride=2)

    for b in range(8):
        value = []
        for a in range(0, 8, 2):
            both = jnp.concatenate([grid[within(8 * (a + i) + b, 0), :] for i in range(2)], axis=1)
            both = left(table_y[...], both)
            value += [both[:, :NZ], both[:, NZ:]]
        for k, part in enumerate(hartley8(value)):
            turned[plane(8 * b + k), :] = part

    def part_of(j):
        return lambda x: pl.ds(pl.multiple_of(x * NY + j * LINES, LINES), LINES)

    @pl.loop(0, NY // LINES)
    def _(j):
        at = part_of(j)
        combine(lambda b, k: turned[at(8 * b + k), :], lambda x, v: work.__setitem__((at(x), slice(None)), v))

    for i in range(NX * NY // ROWS):
        at = pl.ds(i * ROWS, ROWS)
        work[at, :] = along_z(along_z(work[at, :], table_z[...]) * kernel[at, :], table_z[...])

    @pl.loop(0, NY // LINES)
    def _(j):
        at = part_of(j)
        separate(lambda x: work[at(x), :], lambda b, k, v: turned.__setitem__((at(8 * b + k), slice(None)), v))

    for b in range(8):
        value = hartley8([turned[plane(8 * b + k), :] for k in range(8)])
        for a in range(0, 8, 2):
            both = left(table_y[...], jnp.concatenate(value[a:a + 2], axis=1))
            for i in range(2):
                x = 8 * (a + i) + b
                part = both[:, i * NZ:(i + 1) * NZ]
                out[plane(x), :] = (part * grid[within(x, 1), :]).astype(jnp.bfloat16)


def exchange(stick_perm, stick_counts, facts, owned, source, mine):
    sticks, capacity, depth = owned.shape
    table_y, low_y = halves(hartley_table(NY))
    table_z, low_z = halves(hartley_table(NZ))
    left_y = jnp.asarray(np.concatenate([table_y, table_y, low_y], axis=1))
    right_z = np.concatenate(
        [np.concatenate([table_z, low_z], axis=1), np.concatenate([table_z, np.zeros_like(low_z)], axis=1)], axis=0)
    right_z = jnp.asarray(right_z)
    kernel = screened(signed_freq(NX), signed_freq(NY), signed_freq(NZ)) * (-1.0 / (NX * NY * NZ))
    kernel = jnp.asarray(kernel.reshape(NX * NY, NZ), jnp.float32)
    target = jnp.pad(stick_perm * 2, (0, UNIT), constant_values=2 * NX * NY)
    smem = pl.BlockSpec(memory_space=pltpu.SMEM)
    vmem = pl.BlockSpec(memory_space=pltpu.VMEM)
    anywhere = pl.BlockSpec(memory_space=pl.ANY)
    slots = sticks * capacity
    full = lambda n: pltpu.VMEM((n, NZ), jnp.float32)
    return pl.pallas_call(
        functools.partial(exchange_kernel, sticks, capacity),
        out_shape=jax.ShapeDtypeStruct((NX * NY, NZ), jnp.bfloat16),
        in_specs=[smem] * 3 + [anywhere] * 3 + [vmem] * 3,
        out_specs=vmem,
        scratch_shapes=[pltpu.VMEM((slots, NZ), jnp.bfloat16), pltpu.VMEM((slots, NZ), jnp.bfloat16),
                        pltpu.SemaphoreType.DMA((2, sticks)), full(2 * slots), full(2 * NX * NY + 8), full(NX * NY),
                        full(NX * NY)],
        compiler_params=pltpu.CompilerParams(vmem_limit_bytes=40 << 20),
    )(target, stick_counts, facts, owned, source, mine, left_y, right_z, kernel)


def local(orbital_sticks, stick_perm, stick_counts, source_ids):
    sticks = lax.axis_size("stick")
    bands = lax.axis_size("band")
    rows = orbital_sticks.shape[0]
    group = source_ids[0] // rows
    row = source_ids[0] % rows
    lines = bands // (WIDE * CORES)
    if sticks == 2 and lines * WIDE * CORES == bands and bands <= 16 and orbital_sticks.shape[1] % (2 * EACH) == 0:
        branches = [functools.partial(spread, root, lines) for root in range(bands)]
        source, owned = lax.switch(group, branches, source_ids % rows, orbital_sticks)
    else:
        piece = lax.dynamic_index_in_dim(orbital_sticks, row, 0, keepdims=False)
        source, owned = spread_far(group, piece, orbital_sticks)
    is_root = (lax.axis_index("band") == group).astype(jnp.int32)
    facts = jnp.stack([lax.axis_index("stick"), is_root, row]).astype(jnp.int32)
    out = exchange(stick_perm, stick_counts, facts, owned, source, orbital_sticks)
    return out.reshape(1, NX, NY, NZ)


def solution(mesh):
    placed = (P("band", "stick", None), P(), P(), P())
    return jax.shard_map(
        local,
        mesh=mesh,
        in_specs=placed,
        out_specs=P(("band", "stick"), None, None, None),
        check_vma=False,
    )
```

```python
import functools
import math

import jax
import jax.numpy as jnp
import numpy as np
from jax import lax
from jax.experimental import pallas as pl
from jax.experimental.pallas import tpu as pltpu
from jax.sharding import PartitionSpec as P

NX = 64
NY = 64
NZ = 128
EACH = 4
LEVELS = 4
WIDE = 2
CORES = 2
PARTS = 8
SECOND_EARLY = 2
BESIDE_EARLY = 2
LAG = 4
UNIT = 64
SPAN = 256
LINES = 16
ROWS = 512
ROOT = math.sqrt(2.0)
HALF = math.sqrt(0.5)

screen_omega = 0.25


def signed_freq(length):
    steps = np.arange(length, dtype=np.int32)
    signed = np.where(steps <= length // 2, steps, steps - length)
    return signed.astype(np.float64) / length


def screened(freq_x, freq_y, freq_z):
    square = (2.0 * math.pi) ** 2 * (
        freq_x[:, None, None] ** 2 + freq_y[None, :, None] ** 2 + freq_z[None, None, :] ** 2
    )
    safe = np.where(square > 0, square, 1.0)
    inner = 4.0 * math.pi * (1.0 - np.exp(-square / (4.0 * screen_omega**2))) / safe
    return np.where(square > 0, inner, math.pi / screen_omega**2)


def hartley_table(length):
    steps = np.arange(length, dtype=np.int64)
    angle = (steps[:, None] * steps[None, :] % length) * (2.0 * math.pi / length)
    return np.cos(angle) + np.sin(angle)


def halves(table):
    high = table.astype(jnp.bfloat16)
    low = (table - high.astype(np.float64)).astype(jnp.bfloat16)
    return high, low


def tree_of(lines, root):
    middle = 2 if root == 0 else lines - 3 if root == lines - 1 else -1
    if lines == 4 and middle >= 0:
        return {root: [middle], middle: [middle - 1, middle + 1]} if root == 0 else {root: [middle], middle: [middle + 1, middle - 1]}
    tree = {}
    for line in range(lines):
        if line < root:
            tree.setdefault(line + 1, []).append(line)
        if line > root:
            tree.setdefault(line - 1, []).append(line)
    return tree


def spread_kernel(root, lines, live, row, mine, source, owned, stage, piece, stage_sem, send, arrived, swap_send, swap_recv):
    rows = mine.shape[0]
    chunk = live // (2 * EACH)
    length = live // PARTS
    stick = lax.axis_index("stick")
    band = lax.axis_index("band")
    core = band % CORES
    side = (band // CORES) % WIDE
    line = band // (CORES * WIDE)
    root_core = root % CORES
    root_side = (root // CORES) % WIDE
    root_line = root // (CORES * WIDE)
    place = lambda l, r, c: (l * WIDE + r) * CORES + c
    tree = tree_of(lines, root_line)
    is_root = band == root
    half = (core + root_core) % 2
    here = line == root_line
    near = (side + root_side) % 2 == half
    origin = here & near
    second = origin & (half == 1)

    every = pl.ds(0, live)
    fetch = [pltpu.make_async_copy(mine.at[r, every], stage.at[r], stage_sem.at[r]) for r in range(rows)]

    @pl.when(is_root)
    def _():
        for r in range(rows):
            fetch[r].start()

    barrier = pltpu.get_barrier_semaphore()

    def greet(**where):
        pl.semaphore_signal(barrier, inc=1, device_id=where, device_id_type=pl.DeviceIdType.MESH)

    hops = [(parent, child) for parent in sorted(tree) for child in tree[parent]]
    count = 3
    for parent, child in hops:
        pl.when(near & (line == parent))(lambda child=child: greet(band=place(child, side, core)))
        pl.when(near & (line == child))(lambda parent=parent: greet(band=place(parent, side, core)))
        count = count + jnp.where(near & (line == parent), 1, 0) + jnp.where(near & (line == child), 1, 0)
    greet(band=place(line, 1 - side, core))
    greet(band=place(line, side, 1 - core))
    greet(stick=1 - stick)
    pl.when(is_root)(lambda: greet(band=place(root_line, 1 - root_side, 1 - root_core)))
    pl.when(second)(lambda: greet(band=root))
    count = count + jnp.where(is_root, 1, 0) + jnp.where(second, 1, 0)

    @pl.when(is_root)
    def _():
        for r in range(rows):
            fetch[r].wait()

        @pl.loop(0, 2 * EACH)
        def _(q):
            at = pl.ds(pl.multiple_of(q * chunk, chunk), chunk)
            value = stage[0, at, :]
            for r in range(1, rows):
                value = jnp.where(row[0] == r, stage[r, at, :], value)
            piece[at, :] = value

    pl.semaphore_wait(barrier, count)

    def remote(src, dst, sent, came, where):
        return pltpu.make_async_remote_copy(src_ref=src, dst_ref=dst, send_sem=sent, recv_sem=came, device_id=where,
                                            device_id_type=pl.DeviceIdType.MESH)

    def swap(part):
        at = pl.ds(pl.multiple_of(part * length, length), length)
        return remote(mine.at[1 - stick, at], owned.at[stick, at], swap_send.at[part], swap_recv.at[part],
                      dict(stick=1 - stick))

    def copy(slot, block, q, src, **where):
        at = pl.ds(pl.multiple_of(q * chunk, chunk), chunk)
        return remote(src.at[at], source.at[block, at], send.at[slot, block, q], arrived.at[block, q], where)

    beside = place(line, side, 1 - core)
    fan = max(len(children) for children in tree.values())
    to_root = here & (side == root_side) & (half == 1)
    early = lambda part: jnp.logical_not(here) | (second & (part < SECOND_EARLY)) | (here & jnp.logical_not(origin) & (part < BESIDE_EARLY))

    def urgent(block, q, src, own, act):
        if own:
            pl.when(origin)(lambda: act(copy(fan + 2, block, q, src, stick=1 - stick)))
        for parent, children in tree.items():
            for n, child in enumerate(children):
                pl.when(near & (line == parent))(
                    lambda n=n, child=child: act(copy(n, block, q, src, band=place(child, side, core))))

    def patient(block, q, src, own, act):
        pl.when(near)(lambda: act(copy(fan, block, q, src, band=place(line, 1 - side, core))))
        send_beside = lambda: act(copy(fan + 1, block, q, src, band=beside))
        if own:
            pl.when(jnp.logical_not(to_root))(send_beside)
        else:
            send_beside()

    def exits(block, q, src, own, act):
        urgent(block, q, src, own, act)
        patient(block, q, src, own, act)

    def to_second(q, act):
        act(copy(fan + 3, stick, q, piece, band=place(root_line, 1 - root_side, 1 - root_core)))

    def arrive(block, q):
        copy(fan + 1, block, q, source.at[block], band=beside).wait_recv()

    start = lambda job: job.start()
    finish = lambda job: job.wait_send()
    first = half * EACH
    ours, theirs = source.at[stick], source.at[1 - stick]

    @pl.loop(0, PARTS)
    def _(part):
        pl.when(early(part))(lambda: swap(part).start())

    def own_step(i):
        @pl.when(is_root)
        def _():
            to_second(EACH + i, start)
            urgent(stick, i, piece, True, start)

        @pl.when(jnp.logical_not(is_root))
        def _():
            arrive(stick, first + i)
            exits(stick, first + i, ours, True, start)

    def other_step(i):
        arrive(1 - stick, first + i)
        exits(1 - stick, first + i, theirs, False, start)

    @pl.loop(0, LAG)
    def _(i):
        own_step(i)

    if LAG < EACH:
        @pl.loop(LAG, EACH)
        def _(i):
            own_step(i)
            other_step(i - LAG)

    @pl.when(is_root)
    def _():
        @pl.loop(0, EACH)
        def _(i):
            patient(stick, i, piece, True, start)

    @pl.loop(0, PARTS)
    def _(part):
        pl.when(jnp.logical_not(early(part)))(lambda: swap(part).start())

    @pl.loop(EACH - LAG, EACH)
    def _(i):
        other_step(i)

    @pl.loop(0, EACH)
    def _(i):
        q = (1 - half) * EACH + i
        pl.when(jnp.logical_not(is_root))(lambda: arrive(stick, q))
        arrive(1 - stick, q)

    @pl.loop(0, EACH)
    def _(i):
        exits(stick, first + i, ours, True, finish)
        exits(1 - stick, first + i, theirs, False, finish)
        pl.when(is_root)(lambda: to_second(EACH + i, finish))

    @pl.loop(0, PARTS)
    def _(part):
        swap(part).wait()


def spread(root, lines, live, number, row, mine):
    rows, capacity, depth = mine.shape
    dma = pltpu.SemaphoreType.DMA
    block = jax.ShapeDtypeStruct((2, capacity, depth), mine.dtype)
    anywhere = pl.BlockSpec(memory_space=pl.ANY)
    return pl.pallas_call(
        functools.partial(spread_kernel, root, lines, live),
        out_shape=(block, block),
        in_specs=[pl.BlockSpec(memory_space=pltpu.SMEM), anywhere],
        out_specs=(anywhere, anywhere),
        scratch_shapes=[pltpu.VMEM((rows, live, depth), mine.dtype), pltpu.VMEM((live, depth), mine.dtype),
                        dma((rows,)), dma((6, 2, 2 * EACH)), dma((2, 2 * EACH)), dma((PARTS,)), dma((PARTS,))],
        compiler_params=pltpu.CompilerParams(collective_id=number, has_side_effects=True, vmem_limit_bytes=16 << 20),
    )(row, mine)


def spread_far(group, piece, mine):
    is_root = lax.axis_index("band") == group
    piece = lax.psum(jnp.where(is_root, piece, jnp.zeros_like(piece)), "band")
    source = lax.all_gather(piece, "stick", axis=0, tiled=False)
    owned = lax.all_to_all(mine, "stick", split_axis=0, concat_axis=0, tiled=True)
    return source, owned


def split(value):
    high = value.astype(jnp.bfloat16)
    low = (value - high.astype(jnp.float32)).astype(jnp.bfloat16)
    return high, low


def left(table, value):
    high, low = split(value)
    return jnp.dot(table, jnp.concatenate([high, low, high], axis=0), preferred_element_type=jnp.float32)


def along_z(value, table):
    high, low = split(value)
    both = jnp.dot(jnp.concatenate([high, low], axis=1), table, preferred_element_type=jnp.float32)
    return both[:, :NZ] + both[:, NZ:]


def hartley8(x):
    s = [x[i] + x[i + 4] for i in range(4)]
    d = [x[i] - x[i + 4] for i in range(4)]
    p, q, r, u = s[0] + s[2], s[1] + s[3], s[0] - s[2], s[1] - s[3]
    e, f, g, h = d[0] + d[2], d[0] - d[2], d[1] * ROOT, d[3] * ROOT
    return [p + q, e + g, r + u, f + h, p - q, e - g, r - u, f - h]


def plus(a, b):
    return a[0] + b[0], a[1] + b[1]


def minus(a, b):
    return a[0] - b[0], a[1] - b[1]


def fourier4(x, sign):
    a, b, c, d = plus(x[0], x[2]), minus(x[0], x[2]), plus(x[1], x[3]), minus(x[1], x[3])
    ahead, back = (b[0] - d[1], b[1] + d[0]), (b[0] + d[1], b[1] - d[0])
    if sign < 0:
        ahead, back = back, ahead
    return [plus(a, c), ahead, minus(a, c), back]


def fourier8(x, sign):
    even = fourier4([plus(x[i], x[i + 4]) for i in range(4)], sign)
    d = [minus(x[i], x[i + 4]) for i in range(4)]
    (a, b), (p, q), (u, v) = d[1], d[2], d[3]
    if sign > 0:
        turned = [((a - b) * HALF, (a + b) * HALF), (-q, p), ((u + v) * -HALF, (u - v) * HALF)]
    else:
        turned = [((a + b) * HALF, (b - a) * HALF), (q, -p), ((v - u) * HALF, (u + v) * -HALF)]
    odd = fourier4([d[0]] + turned, sign)
    return [value for both in zip(even, odd) for value in both]


def rotate(value, step, sign):
    if step == 0:
        return value
    c, s = math.cos(2 * math.pi * step / NX), sign * math.sin(2 * math.pi * step / NX)
    return value[0] * c - value[1] * s, value[1] * c + value[0] * s


def combine(get, put):
    for k, value in enumerate(hartley8([get(b, 0) for b in range(8)])):
        put(8 * k, value)
    for first in range(1, 4):
        mixed = fourier8([rotate((get(b, first), get(b, 8 - first)), b * first, -1) for b in range(8)], -1)
        for k, (p, q) in enumerate(mixed):
            put(first + 8 * k, p)
            put(NX - first - 8 * k, q)
    mixed = fourier8([rotate((get(b, 4), jnp.zeros_like(get(b, 4))), b * 4, -1) for b in range(8)], -1)
    for k in range(4):
        put(4 + 8 * k, mixed[k][0] - mixed[k][1])
        put(NX - 4 - 8 * k, mixed[k][0] + mixed[k][1])


def separate(get, put):
    for b, value in enumerate(hartley8([get(8 * k) for k in range(8)])):
        put(b, 0, value)
    for first in range(1, 4):
        mixed = fourier8([(get(first + 8 * k), get(NX - first - 8 * k)) for k in range(8)], 1)
        for b in range(8):
            p, q = rotate(mixed[b], b * first, 1)
            put(b, first, p)
            put(b, 8 - first, q)
    mixed = fourier8([(get(4 + 8 * k), jnp.zeros_like(get(4))) for k in range(8)], 1)
    for b in range(8):
        p, q = rotate(mixed[b], b * 4, 1)
        put(b, 4, p + q)


def exchange_kernel(sticks, capacity, target, counts, facts, owned_far, source_far, mine, table_y, table_z,
                    kernel, out, owned, source, sem, slot, grid, turned, work):
    stick, is_root, root_row = facts[0], facts[1], facts[2]
    unit = math.gcd(capacity, UNIT)
    span = math.gcd(capacity, SPAN)

    def fetch(block):
        at = pl.ds(block * capacity, capacity)
        bring = lambda src, dst, which: pltpu.make_async_copy(src, dst.at[at], sem.at[which, block]).start()
        here = block == stick
        pl.when(here)(lambda: bring(mine.at[block], owned, 0))
        pl.when(jnp.logical_not(here))(lambda: bring(owned_far.at[block], owned, 0))
        from_mine = here & (is_root == 1)
        pl.when(from_mine)(lambda: bring(mine.at[root_row], source, 1))
        pl.when(jnp.logical_not(from_mine))(lambda: bring(source_far.at[block], source, 1))

    for block in range(sticks):
        fetch(block)

    offset = 0
    for block in range(sticks):
        count = counts[block]
        base = block * capacity
        at_block = pl.ds(base, capacity)
        pltpu.make_async_copy(owned_far.at[block], owned.at[at_block], sem.at[0, block]).wait()
        pltpu.make_async_copy(source_far.at[block], source.at[at_block], sem.at[1, block]).wait()

        @pl.loop(0, pl.cdiv(count, span))
        def _(i):
            first = pl.multiple_of(base + i * span, span)
            value = source[pl.ds(first, span), :].astype(jnp.float32)
            slot[pl.ds(2 * first, span, stride=2), :] = owned[pl.ds(first, span), :].astype(jnp.float32) * value
            slot[pl.ds(2 * first + 1, span, stride=2), :] = value

        @pl.loop(0, pl.cdiv(count, unit))
        def _(j):
            for u in range(unit):
                i = j * unit + u
                grid[pl.ds(target[offset + i], 2), :] = slot[pl.ds(2 * (base + i), 2), :]

        offset = offset + count

    plane = lambda x: pl.ds(x * NY, NY)
    within = lambda x, which: pl.ds(2 * NY * x + which, NY, stride=2)

    for b in range(8):
        value = []
        for a in range(0, 8, 2):
            both = jnp.concatenate([grid[within(8 * (a + i) + b, 0), :] for i in range(2)], axis=1)
            both = left(table_y[...], both)
            value += [both[:, :NZ], both[:, NZ:]]
        for k, part in enumerate(hartley8(value)):
            turned[plane(8 * b + k), :] = part

    def part_of(j):
        return lambda x: pl.ds(pl.multiple_of(x * NY + j * LINES, LINES), LINES)

    @pl.loop(0, NY // LINES)
    def _(j):
        at = part_of(j)
        combine(lambda b, k: turned[at(8 * b + k), :], lambda x, v: work.__setitem__((at(x), slice(None)), v))

    for i in range(NX * NY // ROWS):
        at = pl.ds(i * ROWS, ROWS)
        work[at, :] = along_z(along_z(work[at, :], table_z[...]) * kernel[at, :], table_z[...])

    @pl.loop(0, NY // LINES)
    def _(j):
        at = part_of(j)
        separate(lambda x: work[at(x), :], lambda b, k, v: turned.__setitem__((at(8 * b + k), slice(None)), v))

    for b in range(8):
        value = hartley8([turned[plane(8 * b + k), :] for k in range(8)])
        for a in range(0, 8, 2):
            both = left(table_y[...], jnp.concatenate(value[a:a + 2], axis=1))
            for i in range(2):
                x = 8 * (a + i) + b
                part = both[:, i * NZ:(i + 1) * NZ]
                out[plane(x), :] = (part * grid[within(x, 1), :]).astype(jnp.bfloat16)


def exchange(stick_perm, stick_counts, facts, owned, source, mine):
    sticks, capacity, depth = owned.shape
    table_y, low_y = halves(hartley_table(NY))
    table_z, low_z = halves(hartley_table(NZ))
    left_y = jnp.asarray(np.concatenate([table_y, table_y, low_y], axis=1))
    right_z = np.concatenate(
        [np.concatenate([table_z, low_z], axis=1), np.concatenate([table_z, np.zeros_like(low_z)], axis=1)], axis=0)
    right_z = jnp.asarray(right_z)
    kernel = screened(signed_freq(NX), signed_freq(NY), signed_freq(NZ)) * (-1.0 / (NX * NY * NZ))
    kernel = jnp.asarray(kernel.reshape(NX * NY, NZ), jnp.float32)
    target = jnp.pad(stick_perm * 2, (0, UNIT), constant_values=2 * NX * NY)
    smem = pl.BlockSpec(memory_space=pltpu.SMEM)
    vmem = pl.BlockSpec(memory_space=pltpu.VMEM)
    anywhere = pl.BlockSpec(memory_space=pl.ANY)
    slots = sticks * capacity
    full = lambda n: pltpu.VMEM((n, NZ), jnp.float32)
    return pl.pallas_call(
        functools.partial(exchange_kernel, sticks, capacity),
        out_shape=jax.ShapeDtypeStruct((NX * NY, NZ), jnp.bfloat16),
        in_specs=[smem] * 3 + [anywhere] * 3 + [vmem] * 3,
        out_specs=vmem,
        scratch_shapes=[pltpu.VMEM((slots, NZ), jnp.bfloat16), pltpu.VMEM((slots, NZ), jnp.bfloat16),
                        pltpu.SemaphoreType.DMA((2, sticks)), full(2 * slots), full(2 * NX * NY + 8), full(NX * NY),
                        full(NX * NY)],
        compiler_params=pltpu.CompilerParams(vmem_limit_bytes=40 << 20),
    )(target, stick_counts, facts, owned, source, mine, left_y, right_z, kernel)


def local(orbital_sticks, stick_perm, stick_counts, source_ids):
    sticks = lax.axis_size("stick")
    bands = lax.axis_size("band")
    rows = orbital_sticks.shape[0]
    group = source_ids[0] // rows
    row = source_ids[0] % rows
    lines = bands // (WIDE * CORES)
    capacity = orbital_sticks.shape[1]
    least = stick_perm.shape[0] // sticks
    step = (capacity - least) // LEVELS
    lives = [least + step * (n + 1) for n in range(LEVELS)]
    fits = lives[-1] == capacity and all(live % (32 * EACH) == 0 and live % (16 * PARTS) == 0 for live in lives)
    if sticks == 2 and lines * WIDE * CORES == bands and bands <= 16 and fits:
        level = jnp.clip((jnp.max(stick_counts) - least + step - 1) // step - 1, 0, LEVELS - 1)
        branches = [functools.partial(spread, root, lines, live, root * LEVELS + n)
                    for root in range(bands) for n, live in enumerate(lives)]
        source, owned = lax.switch(group * LEVELS + level, branches, source_ids % rows, orbital_sticks)
    else:
        piece = lax.dynamic_index_in_dim(orbital_sticks, row, 0, keepdims=False)
        source, owned = spread_far(group, piece, orbital_sticks)
    is_root = (lax.axis_index("band") == group).astype(jnp.int32)
    facts = jnp.stack([lax.axis_index("stick"), is_root, row]).astype(jnp.int32)
    out = exchange(stick_perm, stick_counts, facts, owned, source, orbital_sticks)
    return out.reshape(1, NX, NY, NZ)


def solution(mesh):
    placed = (P("band", "stick", None), P(), P(), P())
    return jax.shard_map(
        local,
        mesh=mesh,
        in_specs=placed,
        out_specs=P(("band", "stick"), None, None, None),
        check_vma=False,
    )
```

```python
import functools
import math

import jax
import jax.numpy as jnp
import numpy as np
from jax import lax
from jax.experimental import pallas as pl
from jax.experimental.pallas import tpu as pltpu
from jax.sharding import PartitionSpec as P

NX = 64
NY = 64
NZ = 128
EACH = 4
WIDE = 2
CORES = 2
PARTS = 8
SECOND_EARLY = 2
BESIDE_EARLY = 2
LAG = 4
UNIT = 64
SPAN = 256
LINES = 16
ROWS = 512
ROOT = math.sqrt(2.0)
HALF = math.sqrt(0.5)

screen_omega = 0.25


def signed_freq(length):
    steps = np.arange(length, dtype=np.int32)
    signed = np.where(steps <= length // 2, steps, steps - length)
    return signed.astype(np.float64) / length


def screened(freq_x, freq_y, freq_z):
    square = (2.0 * math.pi) ** 2 * (
        freq_x[:, None, None] ** 2 + freq_y[None, :, None] ** 2 + freq_z[None, None, :] ** 2
    )
    safe = np.where(square > 0, square, 1.0)
    inner = 4.0 * math.pi * (1.0 - np.exp(-square / (4.0 * screen_omega**2))) / safe
    return np.where(square > 0, inner, math.pi / screen_omega**2)


def hartley_table(length):
    steps = np.arange(length, dtype=np.int64)
    angle = (steps[:, None] * steps[None, :] % length) * (2.0 * math.pi / length)
    return np.cos(angle) + np.sin(angle)


def halves(table):
    high = table.astype(jnp.bfloat16)
    low = (table - high.astype(np.float64)).astype(jnp.bfloat16)
    return high, low


def tree_of(lines, root):
    middle = 2 if root == 0 else lines - 3 if root == lines - 1 else -1
    if lines == 4 and middle >= 0:
        return {root: [middle], middle: [middle - 1, middle + 1]} if root == 0 else {root: [middle], middle: [middle + 1, middle - 1]}
    tree = {}
    for line in range(lines):
        if line < root:
            tree.setdefault(line + 1, []).append(line)
        if line > root:
            tree.setdefault(line - 1, []).append(line)
    return tree


def spread_kernel(root, lines, row, mine, source, owned, stage, piece, stage_sem, send, arrived, swap_send, swap_recv):
    rows, capacity, _ = mine.shape
    chunk = capacity // (2 * EACH)
    length = capacity // PARTS
    stick = lax.axis_index("stick")
    band = lax.axis_index("band")
    core = band % CORES
    side = (band // CORES) % WIDE
    line = band // (CORES * WIDE)
    root_core = root % CORES
    root_side = (root // CORES) % WIDE
    root_line = root // (CORES * WIDE)
    place = lambda l, r, c: (l * WIDE + r) * CORES + c
    tree = tree_of(lines, root_line)
    is_root = band == root
    half = (core + root_core) % 2
    here = line == root_line
    near = (side + root_side) % 2 == half
    origin = here & near
    second = origin & (half == 1)

    fetch = [pltpu.make_async_copy(mine.at[r], stage.at[r], stage_sem.at[r]) for r in range(rows)]

    @pl.when(is_root)
    def _():
        for r in range(rows):
            fetch[r].start()

    barrier = pltpu.get_barrier_semaphore()

    def greet(**where):
        pl.semaphore_signal(barrier, inc=1, device_id=where, device_id_type=pl.DeviceIdType.MESH)

    hops = [(parent, child) for parent in sorted(tree) for child in tree[parent]]
    count = 3
    for parent, child in hops:
        pl.when(near & (line == parent))(lambda child=child: greet(band=place(child, side, core)))
        pl.when(near & (line == child))(lambda parent=parent: greet(band=place(parent, side, core)))
        count = count + jnp.where(near & (line == parent), 1, 0) + jnp.where(near & (line == child), 1, 0)
    greet(band=place(line, 1 - side, core))
    greet(band=place(line, side, 1 - core))
    greet(stick=1 - stick)
    pl.when(is_root)(lambda: greet(band=place(root_line, 1 - root_side, 1 - root_core)))
    pl.when(second)(lambda: greet(band=root))
    count = count + jnp.where(is_root, 1, 0) + jnp.where(second, 1, 0)

    @pl.when(is_root)
    def _():
        for r in range(rows):
            fetch[r].wait()

        @pl.loop(0, 2 * EACH)
        def _(q):
            at = pl.ds(pl.multiple_of(q * chunk, chunk), chunk)
            value = stage[0, at, :]
            for r in range(1, rows):
                value = jnp.where(row[0] == r, stage[r, at, :], value)
            piece[at, :] = value

    pl.semaphore_wait(barrier, count)

    def remote(src, dst, sent, came, where):
        return pltpu.make_async_remote_copy(src_ref=src, dst_ref=dst, send_sem=sent, recv_sem=came, device_id=where,
                                            device_id_type=pl.DeviceIdType.MESH)

    def swap(part):
        at = pl.ds(pl.multiple_of(part * length, length), length)
        return remote(mine.at[1 - stick, at], owned.at[stick, at], swap_send.at[part], swap_recv.at[part],
                      dict(stick=1 - stick))

    def copy(slot, block, q, src, **where):
        at = pl.ds(pl.multiple_of(q * chunk, chunk), chunk)
        return remote(src.at[at], source.at[block, at], send.at[slot, block, q], arrived.at[block, q], where)

    beside = place(line, side, 1 - core)
    fan = max(len(children) for children in tree.values())
    to_root = here & (side == root_side) & (half == 1)
    early = lambda part: jnp.logical_not(here) | (second & (part < SECOND_EARLY)) | (here & jnp.logical_not(origin) & (part < BESIDE_EARLY))

    def urgent(block, q, src, own, act):
        if own:
            pl.when(origin)(lambda: act(copy(fan + 2, block, q, src, stick=1 - stick)))
        for parent, children in tree.items():
            for n, child in enumerate(children):
                pl.when(near & (line == parent))(
                    lambda n=n, child=child: act(copy(n, block, q, src, band=place(child, side, core))))

    def patient(block, q, src, own, act):
        pl.when(near)(lambda: act(copy(fan, block, q, src, band=place(line, 1 - side, core))))
        send_beside = lambda: act(copy(fan + 1, block, q, src, band=beside))
        if own:
            pl.when(jnp.logical_not(to_root))(send_beside)
        else:
            send_beside()

    def exits(block, q, src, own, act):
        urgent(block, q, src, own, act)
        patient(block, q, src, own, act)

    def to_second(q, act):
        act(copy(fan + 3, stick, q, piece, band=place(root_line, 1 - root_side, 1 - root_core)))

    def arrive(block, q):
        copy(fan + 1, block, q, source.at[block], band=beside).wait_recv()

    start = lambda job: job.start()
    finish = lambda job: job.wait_send()
    first = half * EACH
    ours, theirs = source.at[stick], source.at[1 - stick]

    @pl.loop(0, PARTS)
    def _(part):
        pl.when(early(part))(lambda: swap(part).start())

    def own_step(i):
        @pl.when(is_root)
        def _():
            to_second(EACH + i, start)
            urgent(stick, i, piece, True, start)

        @pl.when(jnp.logical_not(is_root))
        def _():
            arrive(stick, first + i)
            exits(stick, first + i, ours, True, start)

    def other_step(i):
        arrive(1 - stick, first + i)
        exits(1 - stick, first + i, theirs, False, start)

    @pl.loop(0, LAG)
    def _(i):
        own_step(i)

    if LAG < EACH:
        @pl.loop(LAG, EACH)
        def _(i):
            own_step(i)
            other_step(i - LAG)

    @pl.when(is_root)
    def _():
        @pl.loop(0, EACH)
        def _(i):
            patient(stick, i, piece, True, start)

    @pl.loop(0, PARTS)
    def _(part):
        pl.when(jnp.logical_not(early(part)))(lambda: swap(part).start())

    @pl.loop(EACH - LAG, EACH)
    def _(i):
        other_step(i)

    @pl.loop(0, EACH)
    def _(i):
        q = (1 - half) * EACH + i
        pl.when(jnp.logical_not(is_root))(lambda: arrive(stick, q))
        arrive(1 - stick, q)

    @pl.loop(0, EACH)
    def _(i):
        exits(stick, first + i, ours, True, finish)
        exits(1 - stick, first + i, theirs, False, finish)
        pl.when(is_root)(lambda: to_second(EACH + i, finish))

    @pl.loop(0, PARTS)
    def _(part):
        swap(part).wait()


def spread(root, lines, row, mine):
    rows, capacity, depth = mine.shape
    dma = pltpu.SemaphoreType.DMA
    block = jax.ShapeDtypeStruct((2, capacity, depth), mine.dtype)
    anywhere = pl.BlockSpec(memory_space=pl.ANY)
    return pl.pallas_call(
        functools.partial(spread_kernel, root, lines),
        out_shape=(block, block),
        in_specs=[pl.BlockSpec(memory_space=pltpu.SMEM), anywhere],
        out_specs=(anywhere, anywhere),
        scratch_shapes=[pltpu.VMEM((rows, capacity, depth), mine.dtype), pltpu.VMEM((capacity, depth), mine.dtype),
                        dma((rows,)), dma((6, 2, 2 * EACH)), dma((2, 2 * EACH)), dma((PARTS,)), dma((PARTS,))],
        compiler_params=pltpu.CompilerParams(collective_id=root, has_side_effects=True, vmem_limit_bytes=16 << 20),
    )(row, mine)


def spread_far(group, piece, mine):
    is_root = lax.axis_index("band") == group
    piece = lax.psum(jnp.where(is_root, piece, jnp.zeros_like(piece)), "band")
    source = lax.all_gather(piece, "stick", axis=0, tiled=False)
    owned = lax.all_to_all(mine, "stick", split_axis=0, concat_axis=0, tiled=True)
    return source, owned


def split(value):
    high = value.astype(jnp.bfloat16)
    low = (value - high.astype(jnp.float32)).astype(jnp.bfloat16)
    return high, low


def left(table, value):
    high, low = split(value)
    return jnp.dot(table, jnp.concatenate([high, low, high], axis=0), preferred_element_type=jnp.float32)


def along_z(value, table):
    high, low = split(value)
    both = jnp.dot(jnp.concatenate([high, low], axis=1), table, preferred_element_type=jnp.float32)
    return both[:, :NZ] + both[:, NZ:]


def hartley8(x):
    s = [x[i] + x[i + 4] for i in range(4)]
    d = [x[i] - x[i + 4] for i in range(4)]
    p, q, r, u = s[0] + s[2], s[1] + s[3], s[0] - s[2], s[1] - s[3]
    e, f, g, h = d[0] + d[2], d[0] - d[2], d[1] * ROOT, d[3] * ROOT
    return [p + q, e + g, r + u, f + h, p - q, e - g, r - u, f - h]


def plus(a, b):
    return a[0] + b[0], a[1] + b[1]


def minus(a, b):
    return a[0] - b[0], a[1] - b[1]


def fourier4(x, sign):
    a, b, c, d = plus(x[0], x[2]), minus(x[0], x[2]), plus(x[1], x[3]), minus(x[1], x[3])
    ahead, back = (b[0] - d[1], b[1] + d[0]), (b[0] + d[1], b[1] - d[0])
    if sign < 0:
        ahead, back = back, ahead
    return [plus(a, c), ahead, minus(a, c), back]


def fourier8(x, sign):
    even = fourier4([plus(x[i], x[i + 4]) for i in range(4)], sign)
    d = [minus(x[i], x[i + 4]) for i in range(4)]
    (a, b), (p, q), (u, v) = d[1], d[2], d[3]
    if sign > 0:
        turned = [((a - b) * HALF, (a + b) * HALF), (-q, p), ((u + v) * -HALF, (u - v) * HALF)]
    else:
        turned = [((a + b) * HALF, (b - a) * HALF), (q, -p), ((v - u) * HALF, (u + v) * -HALF)]
    odd = fourier4([d[0]] + turned, sign)
    return [value for both in zip(even, odd) for value in both]


def rotate(value, step, sign):
    if step == 0:
        return value
    c, s = math.cos(2 * math.pi * step / NX), sign * math.sin(2 * math.pi * step / NX)
    return value[0] * c - value[1] * s, value[1] * c + value[0] * s


def combine(get, put):
    for k, value in enumerate(hartley8([get(b, 0) for b in range(8)])):
        put(8 * k, value)
    for first in range(1, 4):
        mixed = fourier8([rotate((get(b, first), get(b, 8 - first)), b * first, -1) for b in range(8)], -1)
        for k, (p, q) in enumerate(mixed):
            put(first + 8 * k, p)
            put(NX - first - 8 * k, q)
    mixed = fourier8([rotate((get(b, 4), jnp.zeros_like(get(b, 4))), b * 4, -1) for b in range(8)], -1)
    for k in range(4):
        put(4 + 8 * k, mixed[k][0] - mixed[k][1])
        put(NX - 4 - 8 * k, mixed[k][0] + mixed[k][1])


def separate(get, put):
    for b, value in enumerate(hartley8([get(8 * k) for k in range(8)])):
        put(b, 0, value)
    for first in range(1, 4):
        mixed = fourier8([(get(first + 8 * k), get(NX - first - 8 * k)) for k in range(8)], 1)
        for b in range(8):
            p, q = rotate(mixed[b], b * first, 1)
            put(b, first, p)
            put(b, 8 - first, q)
    mixed = fourier8([(get(4 + 8 * k), jnp.zeros_like(get(4))) for k in range(8)], 1)
    for b in range(8):
        p, q = rotate(mixed[b], b * 4, 1)
        put(b, 4, p + q)


def exchange_kernel(sticks, capacity, target, counts, facts, owned_far, source_far, mine, table_y, table_z,
                    kernel, out, owned, source, sem, slot, grid, turned, work):
    stick, is_root, root_row = facts[0], facts[1], facts[2]
    unit = math.gcd(capacity, UNIT)
    span = math.gcd(capacity, SPAN)

    def fetch(block):
        at = pl.ds(block * capacity, capacity)
        bring = lambda src, dst, which: pltpu.make_async_copy(src, dst.at[at], sem.at[which, block]).start()
        here = block == stick
        pl.when(here)(lambda: bring(mine.at[block], owned, 0))
        pl.when(jnp.logical_not(here))(lambda: bring(owned_far.at[block], owned, 0))
        from_mine = here & (is_root == 1)
        pl.when(from_mine)(lambda: bring(mine.at[root_row], source, 1))
        pl.when(jnp.logical_not(from_mine))(lambda: bring(source_far.at[block], source, 1))

    for block in range(sticks):
        fetch(block)

    offset = 0
    for block in range(sticks):
        count = counts[block]
        base = block * capacity
        at_block = pl.ds(base, capacity)
        pltpu.make_async_copy(owned_far.at[block], owned.at[at_block], sem.at[0, block]).wait()
        pltpu.make_async_copy(source_far.at[block], source.at[at_block], sem.at[1, block]).wait()

        @pl.loop(0, pl.cdiv(count, span))
        def _(i):
            first = pl.multiple_of(base + i * span, span)
            value = source[pl.ds(first, span), :].astype(jnp.float32)
            slot[pl.ds(2 * first, span, stride=2), :] = owned[pl.ds(first, span), :].astype(jnp.float32) * value
            slot[pl.ds(2 * first + 1, span, stride=2), :] = value

        @pl.loop(0, pl.cdiv(count, unit))
        def _(j):
            for u in range(unit):
                i = j * unit + u
                grid[pl.ds(target[offset + i], 2), :] = slot[pl.ds(2 * (base + i), 2), :]

        offset = offset + count

    plane = lambda x: pl.ds(x * NY, NY)
    within = lambda x, which: pl.ds(2 * NY * x + which, NY, stride=2)

    for b in range(8):
        value = []
        for a in range(0, 8, 2):
            both = jnp.concatenate([grid[within(8 * (a + i) + b, 0), :] for i in range(2)], axis=1)
            both = left(table_y[...], both)
            value += [both[:, :NZ], both[:, NZ:]]
        for k, part in enumerate(hartley8(value)):
            turned[plane(8 * b + k), :] = part

    def part_of(j):
        return lambda x: pl.ds(pl.multiple_of(x * NY + j * LINES, LINES), LINES)

    @pl.loop(0, NY // LINES)
    def _(j):
        at = part_of(j)
        combine(lambda b, k: turned[at(8 * b + k), :], lambda x, v: work.__setitem__((at(x), slice(None)), v))

    for i in range(NX * NY // ROWS):
        at = pl.ds(i * ROWS, ROWS)
        work[at, :] = along_z(along_z(work[at, :], table_z[...]) * kernel[at, :], table_z[...])

    @pl.loop(0, NY // LINES)
    def _(j):
        at = part_of(j)
        separate(lambda x: work[at(x), :], lambda b, k, v: turned.__setitem__((at(8 * b + k), slice(None)), v))

    for b in range(8):
        value = hartley8([turned[plane(8 * b + k), :] for k in range(8)])
        for a in range(0, 8, 2):
            both = left(table_y[...], jnp.concatenate(value[a:a + 2], axis=1))
            for i in range(2):
                x = 8 * (a + i) + b
                part = both[:, i * NZ:(i + 1) * NZ]
                out[plane(x), :] = (part * grid[within(x, 1), :]).astype(jnp.bfloat16)


def exchange(stick_perm, stick_counts, facts, owned, source, mine):
    sticks, capacity, depth = owned.shape
    table_y, low_y = halves(hartley_table(NY))
    table_z, low_z = halves(hartley_table(NZ))
    left_y = jnp.asarray(np.concatenate([table_y, table_y, low_y], axis=1))
    right_z = np.concatenate(
        [np.concatenate([table_z, low_z], axis=1), np.concatenate([table_z, np.zeros_like(low_z)], axis=1)], axis=0)
    right_z = jnp.asarray(right_z)
    kernel = screened(signed_freq(NX), signed_freq(NY), signed_freq(NZ)) * (-1.0 / (NX * NY * NZ))
    kernel = jnp.asarray(kernel.reshape(NX * NY, NZ), jnp.float32)
    target = jnp.pad(stick_perm * 2, (0, UNIT), constant_values=2 * NX * NY)
    smem = pl.BlockSpec(memory_space=pltpu.SMEM)
    vmem = pl.BlockSpec(memory_space=pltpu.VMEM)
    anywhere = pl.BlockSpec(memory_space=pl.ANY)
    slots = sticks * capacity
    full = lambda n: pltpu.VMEM((n, NZ), jnp.float32)
    return pl.pallas_call(
        functools.partial(exchange_kernel, sticks, capacity),
        out_shape=jax.ShapeDtypeStruct((NX * NY, NZ), jnp.bfloat16),
        in_specs=[smem] * 3 + [anywhere] * 3 + [vmem] * 3,
        out_specs=vmem,
        scratch_shapes=[pltpu.VMEM((slots, NZ), jnp.bfloat16), pltpu.VMEM((slots, NZ), jnp.bfloat16),
                        pltpu.SemaphoreType.DMA((2, sticks)), full(2 * slots), full(2 * NX * NY + 8), full(NX * NY),
                        full(NX * NY)],
        compiler_params=pltpu.CompilerParams(vmem_limit_bytes=40 << 20),
    )(target, stick_counts, facts, owned, source, mine, left_y, right_z, kernel)


def local(orbital_sticks, stick_perm, stick_counts, source_ids):
    sticks = lax.axis_size("stick")
    bands = lax.axis_size("band")
    rows = orbital_sticks.shape[0]
    group = lax.div(source_ids[0], rows)
    row = lax.rem(source_ids[0], rows)
    lines = bands // (WIDE * CORES)
    fits = orbital_sticks.shape[1] % (16 * math.lcm(2 * EACH, PARTS)) == 0
    if sticks == 2 and lines * WIDE * CORES == bands and bands <= 16 and fits:
        branches = [functools.partial(spread, root, lines) for root in range(bands)]
        source, owned = lax.switch(group, branches, lax.rem(source_ids, rows), orbital_sticks)
    else:
        piece = lax.dynamic_index_in_dim(orbital_sticks, row, 0, keepdims=False)
        source, owned = spread_far(group, piece, orbital_sticks)
    is_root = (lax.axis_index("band") == group).astype(jnp.int32)
    facts = jnp.stack([lax.axis_index("stick"), is_root, row]).astype(jnp.int32)
    out = exchange(stick_perm, stick_counts, facts, owned, source, orbital_sticks)
    return out.reshape(1, NX, NY, NZ)


def solution(mesh):
    placed = (P("band", "stick", None), P(), P(), P())
    return jax.shard_map(
        local,
        mesh=mesh,
        in_specs=placed,
        out_specs=P(("band", "stick"), None, None, None),
        check_vma=False,
    )
```

```python
import functools
import math

import jax
import jax.numpy as jnp
import numpy as np
from jax import lax
from jax.experimental import pallas as pl
from jax.experimental.pallas import tpu as pltpu
from jax.sharding import PartitionSpec as P

NX = 64
NY = 64
NZ = 128
EACH = 4
WIDE = 2
CORES = 2
PARTS = 8
SECOND_EARLY = 2
BESIDE_EARLY = 2
LAG = 4
UNIT = 128
PIECES = 4
SPAN = 256
LINES = 16
ROWS = 512
ROOT = math.sqrt(2.0)
HALF = math.sqrt(0.5)

screen_omega = 0.25


def signed_freq(length):
    steps = np.arange(length, dtype=np.int32)
    signed = np.where(steps <= length // 2, steps, steps - length)
    return signed.astype(np.float64) / length


def screened(freq_x, freq_y, freq_z):
    square = (2.0 * math.pi) ** 2 * (
        freq_x[:, None, None] ** 2 + freq_y[None, :, None] ** 2 + freq_z[None, None, :] ** 2
    )
    safe = np.where(square > 0, square, 1.0)
    inner = 4.0 * math.pi * (1.0 - np.exp(-square / (4.0 * screen_omega**2))) / safe
    return np.where(square > 0, inner, math.pi / screen_omega**2)


def hartley_table(length):
    steps = np.arange(length, dtype=np.int64)
    angle = (steps[:, None] * steps[None, :] % length) * (2.0 * math.pi / length)
    return np.cos(angle) + np.sin(angle)


def halves(table):
    high = table.astype(jnp.bfloat16)
    low = (table - high.astype(np.float64)).astype(jnp.bfloat16)
    return high, low


def tree_of(lines, root):
    middle = 2 if root == 0 else lines - 3 if root == lines - 1 else -1
    if lines == 4 and middle >= 0:
        return {root: [middle], middle: [middle - 1, middle + 1]} if root == 0 else {root: [middle], middle: [middle + 1, middle - 1]}
    tree = {}
    for line in range(lines):
        if line < root:
            tree.setdefault(line + 1, []).append(line)
        if line > root:
            tree.setdefault(line - 1, []).append(line)
    return tree


def spread_kernel(root, lines, row, mine, source, owned, stage, piece, stage_sem, send, arrived, swap_send, swap_recv):
    rows, capacity, _ = mine.shape
    chunk = capacity // (2 * EACH)
    length = capacity // PARTS
    stick = lax.axis_index("stick")
    band = lax.axis_index("band")
    core = band % CORES
    side = (band // CORES) % WIDE
    line = band // (CORES * WIDE)
    root_core = root % CORES
    root_side = (root // CORES) % WIDE
    root_line = root // (CORES * WIDE)
    place = lambda l, r, c: (l * WIDE + r) * CORES + c
    tree = tree_of(lines, root_line)
    is_root = band == root
    half = (core + root_core) % 2
    here = line == root_line
    near = (side + root_side) % 2 == half
    origin = here & near
    second = origin & (half == 1)

    fetch = [pltpu.make_async_copy(mine.at[r], stage.at[r], stage_sem.at[r]) for r in range(rows)]

    @pl.when(is_root)
    def _():
        for r in range(rows):
            fetch[r].start()

    barrier = pltpu.get_barrier_semaphore()

    def greet(**where):
        pl.semaphore_signal(barrier, inc=1, device_id=where, device_id_type=pl.DeviceIdType.MESH)

    hops = [(parent, child) for parent in sorted(tree) for child in tree[parent]]
    count = 3
    for parent, child in hops:
        pl.when(near & (line == parent))(lambda child=child: greet(band=place(child, side, core)))
        pl.when(near & (line == child))(lambda parent=parent: greet(band=place(parent, side, core)))
        count = count + jnp.where(near & (line == parent), 1, 0) + jnp.where(near & (line == child), 1, 0)
    greet(band=place(line, 1 - side, core))
    greet(band=place(line, side, 1 - core))
    greet(stick=1 - stick)
    pl.when(is_root)(lambda: greet(band=place(root_line, 1 - root_side, 1 - root_core)))
    pl.when(second)(lambda: greet(band=root))
    count = count + jnp.where(is_root, 1, 0) + jnp.where(second, 1, 0)

    @pl.when(is_root)
    def _():
        for r in range(rows):
            fetch[r].wait()

        @pl.loop(0, 2 * EACH)
        def _(q):
            at = pl.ds(pl.multiple_of(q * chunk, chunk), chunk)
            value = stage[0, at, :]
            for r in range(1, rows):
                value = jnp.where(row[0] == r, stage[r, at, :], value)
            piece[at, :] = value

    pl.semaphore_wait(barrier, count)

    def remote(src, dst, sent, came, where):
        return pltpu.make_async_remote_copy(src_ref=src, dst_ref=dst, send_sem=sent, recv_sem=came, device_id=where,
                                            device_id_type=pl.DeviceIdType.MESH)

    def swap(part):
        at = pl.ds(pl.multiple_of(part * length, length), length)
        return remote(mine.at[1 - stick, at], owned.at[stick, at], swap_send.at[part], swap_recv.at[part],
                      dict(stick=1 - stick))

    def copy(slot, block, q, src, **where):
        at = pl.ds(pl.multiple_of(q * chunk, chunk), chunk)
        return remote(src.at[at], source.at[block, at], send.at[slot, block, q], arrived.at[block, q], where)

    beside = place(line, side, 1 - core)
    fan = max(len(children) for children in tree.values())
    to_root = here & (side == root_side) & (half == 1)
    early = lambda part: jnp.logical_not(here) | (second & (part < SECOND_EARLY)) | (here & jnp.logical_not(origin) & (part < BESIDE_EARLY))

    def urgent(block, q, src, own, act):
        if own:
            pl.when(origin)(lambda: act(copy(fan + 2, block, q, src, stick=1 - stick)))
        for parent, children in tree.items():
            for n, child in enumerate(children):
                pl.when(near & (line == parent))(
                    lambda n=n, child=child: act(copy(n, block, q, src, band=place(child, side, core))))

    def patient(block, q, src, own, act):
        pl.when(near)(lambda: act(copy(fan, block, q, src, band=place(line, 1 - side, core))))
        send_beside = lambda: act(copy(fan + 1, block, q, src, band=beside))
        if own:
            pl.when(jnp.logical_not(to_root))(send_beside)
        else:
            send_beside()

    def exits(block, q, src, own, act):
        urgent(block, q, src, own, act)
        patient(block, q, src, own, act)

    def to_second(q, act):
        act(copy(fan + 3, stick, q, piece, band=place(root_line, 1 - root_side, 1 - root_core)))

    def arrive(block, q):
        copy(fan + 1, block, q, source.at[block], band=beside).wait_recv()

    start = lambda job: job.start()
    finish = lambda job: job.wait_send()
    first = half * EACH
    ours, theirs = source.at[stick], source.at[1 - stick]

    @pl.loop(0, PARTS)
    def _(part):
        pl.when(early(part))(lambda: swap(part).start())

    def own_step(i):
        @pl.when(is_root)
        def _():
            to_second(EACH + i, start)
            urgent(stick, i, piece, True, start)

        @pl.when(jnp.logical_not(is_root))
        def _():
            arrive(stick, first + i)
            exits(stick, first + i, ours, True, start)

    def other_step(i):
        arrive(1 - stick, first + i)
        exits(1 - stick, first + i, theirs, False, start)

    @pl.loop(0, LAG)
    def _(i):
        own_step(i)

    if LAG < EACH:
        @pl.loop(LAG, EACH)
        def _(i):
            own_step(i)
            other_step(i - LAG)

    @pl.when(is_root)
    def _():
        @pl.loop(0, EACH)
        def _(i):
            patient(stick, i, piece, True, start)

    @pl.loop(0, PARTS)
    def _(part):
        pl.when(jnp.logical_not(early(part)))(lambda: swap(part).start())

    @pl.loop(EACH - LAG, EACH)
    def _(i):
        other_step(i)

    @pl.loop(0, EACH)
    def _(i):
        q = (1 - half) * EACH + i
        pl.when(jnp.logical_not(is_root))(lambda: arrive(stick, q))
        arrive(1 - stick, q)

    @pl.loop(0, EACH)
    def _(i):
        exits(stick, first + i, ours, True, finish)
        exits(1 - stick, first + i, theirs, False, finish)
        pl.when(is_root)(lambda: to_second(EACH + i, finish))

    @pl.loop(0, PARTS)
    def _(part):
        swap(part).wait()


def spread(root, lines, row, mine):
    rows, capacity, depth = mine.shape
    dma = pltpu.SemaphoreType.DMA
    block = jax.ShapeDtypeStruct((2, capacity, depth), mine.dtype)
    anywhere = pl.BlockSpec(memory_space=pl.ANY)
    return pl.pallas_call(
        functools.partial(spread_kernel, root, lines),
        out_shape=(block, block),
        in_specs=[pl.BlockSpec(memory_space=pltpu.SMEM), anywhere],
        out_specs=(anywhere, anywhere),
        scratch_shapes=[pltpu.VMEM((rows, capacity, depth), mine.dtype), pltpu.VMEM((capacity, depth), mine.dtype),
                        dma((rows,)), dma((6, 2, 2 * EACH)), dma((2, 2 * EACH)), dma((PARTS,)), dma((PARTS,))],
        compiler_params=pltpu.CompilerParams(collective_id=root, has_side_effects=True, vmem_limit_bytes=16 << 20),
    )(row, mine)


def spread_far(group, piece, mine):
    is_root = lax.axis_index("band") == group
    piece = lax.psum(jnp.where(is_root, piece, jnp.zeros_like(piece)), "band")
    source = lax.all_gather(piece, "stick", axis=0, tiled=False)
    owned = lax.all_to_all(mine, "stick", split_axis=0, concat_axis=0, tiled=True)
    return source, owned


def split(value):
    high = value.astype(jnp.bfloat16)
    low = (value - high.astype(jnp.float32)).astype(jnp.bfloat16)
    return high, low


def left(table, value):
    high, low = split(value)
    return jnp.dot(table, jnp.concatenate([high, low, high], axis=0), preferred_element_type=jnp.float32)


def along_z(value, table):
    high, low = split(value)
    both = jnp.dot(jnp.concatenate([high, low], axis=1), table, preferred_element_type=jnp.float32)
    return both[:, :NZ] + both[:, NZ:]


def hartley8(x):
    s = [x[i] + x[i + 4] for i in range(4)]
    d = [x[i] - x[i + 4] for i in range(4)]
    p, q, r, u = s[0] + s[2], s[1] + s[3], s[0] - s[2], s[1] - s[3]
    e, f, g, h = d[0] + d[2], d[0] - d[2], d[1] * ROOT, d[3] * ROOT
    return [p + q, e + g, r + u, f + h, p - q, e - g, r - u, f - h]


def plus(a, b):
    return a[0] + b[0], a[1] + b[1]


def minus(a, b):
    return a[0] - b[0], a[1] - b[1]


def fourier4(x, sign):
    a, b, c, d = plus(x[0], x[2]), minus(x[0], x[2]), plus(x[1], x[3]), minus(x[1], x[3])
    ahead, back = (b[0] - d[1], b[1] + d[0]), (b[0] + d[1], b[1] - d[0])
    if sign < 0:
        ahead, back = back, ahead
    return [plus(a, c), ahead, minus(a, c), back]


def fourier8(x, sign):
    even = fourier4([plus(x[i], x[i + 4]) for i in range(4)], sign)
    d = [minus(x[i], x[i + 4]) for i in range(4)]
    (a, b), (p, q), (u, v) = d[1], d[2], d[3]
    if sign > 0:
        turned = [((a - b) * HALF, (a + b) * HALF), (-q, p), ((u + v) * -HALF, (u - v) * HALF)]
    else:
        turned = [((a + b) * HALF, (b - a) * HALF), (q, -p), ((v - u) * HALF, (u + v) * -HALF)]
    odd = fourier4([d[0]] + turned, sign)
    return [value for both in zip(even, odd) for value in both]


def rotate(value, step, sign):
    if step == 0:
        return value
    c, s = math.cos(2 * math.pi * step / NX), sign * math.sin(2 * math.pi * step / NX)
    return value[0] * c - value[1] * s, value[1] * c + value[0] * s


def combine(get, put):
    for k, value in enumerate(hartley8([get(b, 0) for b in range(8)])):
        put(8 * k, value)
    for first in range(1, 4):
        mixed = fourier8([rotate((get(b, first), get(b, 8 - first)), b * first, -1) for b in range(8)], -1)
        for k, (p, q) in enumerate(mixed):
            put(first + 8 * k, p)
            put(NX - first - 8 * k, q)
    mixed = fourier8([rotate((get(b, 4), jnp.zeros_like(get(b, 4))), b * 4, -1) for b in range(8)], -1)
    for k in range(4):
        put(4 + 8 * k, mixed[k][0] - mixed[k][1])
        put(NX - 4 - 8 * k, mixed[k][0] + mixed[k][1])


def separate(get, put):
    for b, value in enumerate(hartley8([get(8 * k) for k in range(8)])):
        put(b, 0, value)
    for first in range(1, 4):
        mixed = fourier8([(get(first + 8 * k), get(NX - first - 8 * k)) for k in range(8)], 1)
        for b in range(8):
            p, q = rotate(mixed[b], b * first, 1)
            put(b, first, p)
            put(b, 8 - first, q)
    mixed = fourier8([(get(4 + 8 * k), jnp.zeros_like(get(4))) for k in range(8)], 1)
    for b in range(8):
        p, q = rotate(mixed[b], b * 4, 1)
        put(b, 4, p + q)


def exchange_kernel(sticks, capacity, target, counts, facts, owned_far, source_far, mine, table_y, table_z,
                    kernel, out, owned, source, sem, slot, grid, turned, work, result, out_sem):
    stick, is_root, root_row = facts[0], facts[1], facts[2]
    length = capacity // PIECES
    unit = math.gcd(length, UNIT)
    span = math.gcd(length, SPAN)

    def fetch(block, piece):
        at = pl.ds(piece * length, length)
        here = block == stick
        from_mine = here & (is_root == 1)

        def bring(src, dst, which):
            pltpu.make_async_copy(src.at[at], dst.at[pl.ds(block * capacity + piece * length, length)],
                                  sem.at[which, block, piece]).start()

        pl.when(here)(lambda: bring(mine.at[block], owned, 0))
        pl.when(jnp.logical_not(here))(lambda: bring(owned_far.at[block], owned, 0))
        pl.when(from_mine)(lambda: bring(mine.at[root_row], source, 1))
        pl.when(jnp.logical_not(from_mine))(lambda: bring(source_far.at[block], source, 1))

    for block in range(sticks):
        for piece in range(PIECES):
            fetch(block, piece)

    offset = 0
    for block in range(sticks):
        for piece in range(PIECES):
            base = block * capacity + piece * length
            at = pl.ds(base, length)
            live = jnp.clip(counts[block] - piece * length, 0, length)
            start = offset + piece * length
            pltpu.make_async_copy(owned_far.at[0, pl.ds(0, length)], owned.at[at], sem.at[0, block, piece]).wait()
            pltpu.make_async_copy(source_far.at[0, pl.ds(0, length)], source.at[at], sem.at[1, block, piece]).wait()

            @pl.loop(0, pl.cdiv(live, span))
            def _(i):
                first = pl.multiple_of(base + i * span, span)
                value = source[pl.ds(first, span), :].astype(jnp.float32)
                slot[pl.ds(2 * first, span, stride=2), :] = owned[pl.ds(first, span), :].astype(jnp.float32) * value
                slot[pl.ds(2 * first + 1, span, stride=2), :] = value

            @pl.loop(0, pl.cdiv(live, unit))
            def _(j):
                for u in range(unit):
                    i = j * unit + u
                    grid[pl.ds(target[start + i], 2), :] = slot[pl.ds(2 * (base + i), 2), :]

        offset = offset + counts[block]

    plane = lambda x: pl.ds(x * NY, NY)
    within = lambda x, which: pl.ds(2 * NY * x + which, NY, stride=2)

    for b in range(8):
        value = []
        for a in range(0, 8, 2):
            both = jnp.concatenate([grid[within(8 * (a + i) + b, 0), :] for i in range(2)], axis=1)
            both = left(table_y[...], both)
            value += [both[:, :NZ], both[:, NZ:]]
        for k, part in enumerate(hartley8(value)):
            turned[plane(8 * b + k), :] = part

    def part_of(j):
        return lambda x: pl.ds(pl.multiple_of(x * NY + j * LINES, LINES), LINES)

    @pl.loop(0, NY // LINES)
    def _(j):
        at = part_of(j)
        combine(lambda b, k: turned[at(8 * b + k), :], lambda x, v: work.__setitem__((at(x), slice(None)), v))

    for i in range(NX * NY // ROWS):
        at = pl.ds(i * ROWS, ROWS)
        work[at, :] = along_z(along_z(work[at, :], table_z[...]) * kernel[at, :], table_z[...])

    @pl.loop(0, NY // LINES)
    def _(j):
        at = part_of(j)
        separate(lambda x: work[at(x), :], lambda b, k, v: turned.__setitem__((at(8 * b + k), slice(None)), v))

    sends = [pltpu.make_async_copy(result.at[:, b], out.at[:, b], out_sem.at[b]) for b in range(8)]
    for b in range(8):
        value = hartley8([turned[plane(8 * b + k), :] for k in range(8)])
        for a in range(0, 8, 2):
            both = left(table_y[...], jnp.concatenate(value[a:a + 2], axis=1))
            for i in range(2):
                x = 8 * (a + i) + b
                part = both[:, i * NZ:(i + 1) * NZ]
                result[a + i, b] = (part * grid[within(x, 1), :]).astype(jnp.bfloat16)
        sends[b].start()
    for copy in sends:
        copy.wait()


def exchange(stick_perm, stick_counts, facts, owned, source, mine):
    sticks, capacity, depth = owned.shape
    table_y, low_y = halves(hartley_table(NY))
    table_z, low_z = halves(hartley_table(NZ))
    left_y = jnp.asarray(np.concatenate([table_y, table_y, low_y], axis=1))
    right_z = np.concatenate(
        [np.concatenate([table_z, low_z], axis=1), np.concatenate([table_z, np.zeros_like(low_z)], axis=1)], axis=0)
    right_z = jnp.asarray(right_z)
    kernel = screened(signed_freq(NX), signed_freq(NY), signed_freq(NZ)) * (-1.0 / (NX * NY * NZ))
    kernel = jnp.asarray(kernel.reshape(NX * NY, NZ), jnp.float32)
    target = jnp.pad(stick_perm * 2, (0, UNIT), constant_values=2 * NX * NY)
    smem = pl.BlockSpec(memory_space=pltpu.SMEM)
    vmem = pl.BlockSpec(memory_space=pltpu.VMEM)
    anywhere = pl.BlockSpec(memory_space=pl.ANY)
    slots = sticks * capacity
    full = lambda n: pltpu.VMEM((n, NZ), jnp.float32)
    return pl.pallas_call(
        functools.partial(exchange_kernel, sticks, capacity),
        out_shape=jax.ShapeDtypeStruct((NX // 8, 8, NY, NZ), jnp.bfloat16),
        in_specs=[smem] * 3 + [anywhere] * 3 + [vmem] * 3,
        out_specs=anywhere,
        scratch_shapes=[pltpu.VMEM((slots, NZ), jnp.bfloat16), pltpu.VMEM((slots, NZ), jnp.bfloat16),
                        pltpu.SemaphoreType.DMA((2, sticks, PIECES)), full(2 * slots), full(2 * NX * NY + 8), full(NX * NY),
                        full(NX * NY), pltpu.VMEM((NX // 8, 8, NY, NZ), jnp.bfloat16), pltpu.SemaphoreType.DMA((8,))],
        compiler_params=pltpu.CompilerParams(vmem_limit_bytes=40 << 20),
    )(target, stick_counts, facts, owned, source, mine, left_y, right_z, kernel)


def local(orbital_sticks, stick_perm, stick_counts, source_ids):
    sticks = lax.axis_size("stick")
    bands = lax.axis_size("band")
    rows = orbital_sticks.shape[0]
    group = lax.div(source_ids[0], rows)
    row = lax.rem(source_ids[0], rows)
    lines = bands // (WIDE * CORES)
    fits = orbital_sticks.shape[1] % (16 * math.lcm(2 * EACH, PARTS)) == 0
    if sticks == 2 and lines * WIDE * CORES == bands and bands <= 16 and fits:
        branches = [functools.partial(spread, root, lines) for root in range(bands)]
        source, owned = lax.switch(group, branches, lax.rem(source_ids, rows), orbital_sticks)
    else:
        piece = lax.dynamic_index_in_dim(orbital_sticks, row, 0, keepdims=False)
        source, owned = spread_far(group, piece, orbital_sticks)
    is_root = (lax.axis_index("band") == group).astype(jnp.int32)
    facts = jnp.stack([lax.axis_index("stick"), is_root, row]).astype(jnp.int32)
    out = exchange(stick_perm, stick_counts, facts, owned, source, orbital_sticks)
    return out.reshape(1, NX, NY, NZ)


def solution(mesh):
    placed = (P("band", "stick", None), P(), P(), P())
    return jax.shard_map(
        local,
        mesh=mesh,
        in_specs=placed,
        out_specs=P(("band", "stick"), None, None, None),
        check_vma=False,
    )
```

```python
import functools
import math

import jax
import jax.numpy as jnp
import numpy as np
from jax import lax
from jax.experimental import pallas as pl
from jax.experimental.pallas import tpu as pltpu
from jax.sharding import PartitionSpec as P

NX = 64
NY = 64
NZ = 128
EACH = 4
WIDE = 2
CORES = 2
PARTS = 4
SECOND_EARLY = 1
BESIDE_EARLY = 1
LAG = 4
UNIT = 128
PIECES = 4
SPAN = 256
LINES = 16
ROWS = 512
ROOT = math.sqrt(2.0)
HALF = math.sqrt(0.5)

screen_omega = 0.25


def signed_freq(length):
    steps = np.arange(length, dtype=np.int32)
    signed = np.where(steps <= length // 2, steps, steps - length)
    return signed.astype(np.float64) / length


def screened(freq_x, freq_y, freq_z):
    square = (2.0 * math.pi) ** 2 * (
        freq_x[:, None, None] ** 2 + freq_y[None, :, None] ** 2 + freq_z[None, None, :] ** 2
    )
    safe = np.where(square > 0, square, 1.0)
    inner = 4.0 * math.pi * (1.0 - np.exp(-square / (4.0 * screen_omega**2))) / safe
    return np.where(square > 0, inner, math.pi / screen_omega**2)


def hartley_table(length):
    steps = np.arange(length, dtype=np.int64)
    angle = (steps[:, None] * steps[None, :] % length) * (2.0 * math.pi / length)
    return np.cos(angle) + np.sin(angle)


def halves(table):
    high = table.astype(jnp.bfloat16)
    low = (table - high.astype(np.float64)).astype(jnp.bfloat16)
    return high, low


def tree_of(lines, root):
    middle = 2 if root == 0 else lines - 3 if root == lines - 1 else -1
    if lines == 4 and middle >= 0:
        return {root: [middle], middle: [middle - 1, middle + 1]} if root == 0 else {root: [middle], middle: [middle + 1, middle - 1]}
    tree = {}
    for line in range(lines):
        if line < root:
            tree.setdefault(line + 1, []).append(line)
        if line > root:
            tree.setdefault(line - 1, []).append(line)
    return tree


def spread_kernel(root, lines, row, mine, source, owned, stage, piece, stage_sem, send, arrived, swap_send, swap_recv):
    rows, capacity, _ = mine.shape
    chunk = capacity // (2 * EACH)
    length = capacity // PARTS
    stick = lax.axis_index("stick")
    band = lax.axis_index("band")
    core = band % CORES
    side = (band // CORES) % WIDE
    line = band // (CORES * WIDE)
    root_core = root % CORES
    root_side = (root // CORES) % WIDE
    root_line = root // (CORES * WIDE)
    place = lambda l, r, c: (l * WIDE + r) * CORES + c
    tree = tree_of(lines, root_line)
    is_root = band == root
    half = (core + root_core) % 2
    here = line == root_line
    near = (side + root_side) % 2 == half
    origin = here & near
    second = origin & (half == 1)

    fetch = [pltpu.make_async_copy(mine.at[r], stage.at[r], stage_sem.at[r]) for r in range(rows)]

    @pl.when(is_root)
    def _():
        for r in range(rows):
            fetch[r].start()

    barrier = pltpu.get_barrier_semaphore()

    def greet(**where):
        pl.semaphore_signal(barrier, inc=1, device_id=where, device_id_type=pl.DeviceIdType.MESH)

    hops = [(parent, child) for parent in sorted(tree) for child in tree[parent]]
    count = 3
    for parent, child in hops:
        pl.when(near & (line == parent))(lambda child=child: greet(band=place(child, side, core)))
        pl.when(near & (line == child))(lambda parent=parent: greet(band=place(parent, side, core)))
        count = count + jnp.where(near & (line == parent), 1, 0) + jnp.where(near & (line == child), 1, 0)
    greet(band=place(line, 1 - side, core))
    greet(band=place(line, side, 1 - core))
    greet(stick=1 - stick)
    pl.when(is_root)(lambda: greet(band=place(root_line, 1 - root_side, 1 - root_core)))
    pl.when(second)(lambda: greet(band=root))
    count = count + jnp.where(is_root, 1, 0) + jnp.where(second, 1, 0)

    @pl.when(is_root)
    def _():
        for r in range(rows):
            fetch[r].wait()

        @pl.loop(0, 2 * EACH)
        def _(q):
            at = pl.ds(pl.multiple_of(q * chunk, chunk), chunk)
            value = stage[0, at, :]
            for r in range(1, rows):
                value = jnp.where(row[0] == r, stage[r, at, :], value)
            piece[at, :] = value

    pl.semaphore_wait(barrier, count)

    def remote(src, dst, sent, came, where):
        return pltpu.make_async_remote_copy(src_ref=src, dst_ref=dst, send_sem=sent, recv_sem=came, device_id=where,
                                            device_id_type=pl.DeviceIdType.MESH)

    def swap(part):
        at = pl.ds(pl.multiple_of(part * length, length), length)
        return remote(mine.at[1 - stick, at], owned.at[stick, at], swap_send.at[part], swap_recv.at[part],
                      dict(stick=1 - stick))

    def copy(slot, block, q, src, **where):
        at = pl.ds(pl.multiple_of(q * chunk, chunk), chunk)
        return remote(src.at[at], source.at[block, at], send.at[slot, block, q], arrived.at[block, q], where)

    beside = place(line, side, 1 - core)
    fan = max(len(children) for children in tree.values())
    to_root = here & (side == root_side) & (half == 1)
    early = lambda part: jnp.logical_not(here) | (second & (part < SECOND_EARLY)) | (here & jnp.logical_not(origin) & (part < BESIDE_EARLY))

    def urgent(block, q, src, own, act):
        if own:
            pl.when(origin)(lambda: act(copy(fan + 2, block, q, src, stick=1 - stick)))
        for parent, children in tree.items():
            for n, child in enumerate(children):
                pl.when(near & (line == parent))(
                    lambda n=n, child=child: act(copy(n, block, q, src, band=place(child, side, core))))

    def patient(block, q, src, own, act):
        pl.when(near)(lambda: act(copy(fan, block, q, src, band=place(line, 1 - side, core))))
        send_beside = lambda: act(copy(fan + 1, block, q, src, band=beside))
        if own:
            pl.when(jnp.logical_not(to_root))(send_beside)
        else:
            send_beside()

    def exits(block, q, src, own, act):
        urgent(block, q, src, own, act)
        patient(block, q, src, own, act)

    def to_second(q, act):
        act(copy(fan + 3, stick, q, piece, band=place(root_line, 1 - root_side, 1 - root_core)))

    def arrive(block, q):
        copy(fan + 1, block, q, source.at[block], band=beside).wait_recv()

    start = lambda job: job.start()
    finish = lambda job: job.wait_send()
    first = half * EACH
    ours, theirs = source.at[stick], source.at[1 - stick]

    @pl.loop(0, PARTS)
    def _(part):
        pl.when(early(part))(lambda: swap(part).start())

    def own_step(i):
        @pl.when(is_root)
        def _():
            to_second(EACH + i, start)
            urgent(stick, i, piece, True, start)

        @pl.when(jnp.logical_not(is_root))
        def _():
            arrive(stick, first + i)
            exits(stick, first + i, ours, True, start)

    def other_step(i):
        arrive(1 - stick, first + i)
        exits(1 - stick, first + i, theirs, False, start)

    @pl.loop(0, LAG)
    def _(i):
        own_step(i)

    if LAG < EACH:
        @pl.loop(LAG, EACH)
        def _(i):
            own_step(i)
            other_step(i - LAG)

    @pl.when(is_root)
    def _():
        @pl.loop(0, EACH)
        def _(i):
            patient(stick, i, piece, True, start)

    @pl.loop(0, PARTS)
    def _(part):
        pl.when(jnp.logical_not(early(part)))(lambda: swap(part).start())

    @pl.loop(EACH - LAG, EACH)
    def _(i):
        other_step(i)

    @pl.loop(0, EACH)
    def _(i):
        q = (1 - half) * EACH + i
        pl.when(jnp.logical_not(is_root))(lambda: arrive(stick, q))
        arrive(1 - stick, q)

    @pl.loop(0, EACH)
    def _(i):
        exits(stick, first + i, ours, True, finish)
        exits(1 - stick, first + i, theirs, False, finish)
        pl.when(is_root)(lambda: to_second(EACH + i, finish))

    @pl.loop(0, PARTS)
    def _(part):
        swap(part).wait()


def spread(root, lines, row, mine):
    rows, capacity, depth = mine.shape
    dma = pltpu.SemaphoreType.DMA
    block = jax.ShapeDtypeStruct((2, capacity, depth), mine.dtype)
    anywhere = pl.BlockSpec(memory_space=pl.ANY)
    return pl.pallas_call(
        functools.partial(spread_kernel, root, lines),
        out_shape=(block, block),
        in_specs=[pl.BlockSpec(memory_space=pltpu.SMEM), anywhere],
        out_specs=(anywhere, anywhere),
        scratch_shapes=[pltpu.VMEM((rows, capacity, depth), mine.dtype), pltpu.VMEM((capacity, depth), mine.dtype),
                        dma((rows,)), dma((6, 2, 2 * EACH)), dma((2, 2 * EACH)), dma((PARTS,)), dma((PARTS,))],
        compiler_params=pltpu.CompilerParams(collective_id=root, has_side_effects=True, vmem_limit_bytes=16 << 20),
    )(row, mine)


def spread_far(group, piece, mine):
    is_root = lax.axis_index("band") == group
    piece = lax.psum(jnp.where(is_root, piece, jnp.zeros_like(piece)), "band")
    source = lax.all_gather(piece, "stick", axis=0, tiled=False)
    owned = lax.all_to_all(mine, "stick", split_axis=0, concat_axis=0, tiled=True)
    return source, owned


def split(value):
    high = value.astype(jnp.bfloat16)
    low = (value - high.astype(jnp.float32)).astype(jnp.bfloat16)
    return high, low


def left(table, value):
    high, low = split(value)
    return jnp.dot(table, jnp.concatenate([high, low, high], axis=0), preferred_element_type=jnp.float32)


def along_z(value, table):
    high, low = split(value)
    both = jnp.dot(jnp.concatenate([high, low], axis=1), table, preferred_element_type=jnp.float32)
    return both[:, :NZ] + both[:, NZ:]


def hartley8(x):
    s = [x[i] + x[i + 4] for i in range(4)]
    d = [x[i] - x[i + 4] for i in range(4)]
    p, q, r, u = s[0] + s[2], s[1] + s[3], s[0] - s[2], s[1] - s[3]
    e, f, g, h = d[0] + d[2], d[0] - d[2], d[1] * ROOT, d[3] * ROOT
    return [p + q, e + g, r + u, f + h, p - q, e - g, r - u, f - h]


def plus(a, b):
    return a[0] + b[0], a[1] + b[1]


def minus(a, b):
    return a[0] - b[0], a[1] - b[1]


def fourier4(x, sign):
    a, b, c, d = plus(x[0], x[2]), minus(x[0], x[2]), plus(x[1], x[3]), minus(x[1], x[3])
    ahead, back = (b[0] - d[1], b[1] + d[0]), (b[0] + d[1], b[1] - d[0])
    if sign < 0:
        ahead, back = back, ahead
    return [plus(a, c), ahead, minus(a, c), back]


def fourier8(x, sign):
    even = fourier4([plus(x[i], x[i + 4]) for i in range(4)], sign)
    d = [minus(x[i], x[i + 4]) for i in range(4)]
    (a, b), (p, q), (u, v) = d[1], d[2], d[3]
    if sign > 0:
        turned = [((a - b) * HALF, (a + b) * HALF), (-q, p), ((u + v) * -HALF, (u - v) * HALF)]
    else:
        turned = [((a + b) * HALF, (b - a) * HALF), (q, -p), ((v - u) * HALF, (u + v) * -HALF)]
    odd = fourier4([d[0]] + turned, sign)
    return [value for both in zip(even, odd) for value in both]


def rotate(value, step, sign):
    if step == 0:
        return value
    c, s = math.cos(2 * math.pi * step / NX), sign * math.sin(2 * math.pi * step / NX)
    return value[0] * c - value[1] * s, value[1] * c + value[0] * s


def combine(get, put):
    for k, value in enumerate(hartley8([get(b, 0) for b in range(8)])):
        put(8 * k, value)
    for first in range(1, 4):
        mixed = fourier8([rotate((get(b, first), get(b, 8 - first)), b * first, -1) for b in range(8)], -1)
        for k, (p, q) in enumerate(mixed):
            put(first + 8 * k, p)
            put(NX - first - 8 * k, q)
    mixed = fourier8([rotate((get(b, 4), jnp.zeros_like(get(b, 4))), b * 4, -1) for b in range(8)], -1)
    for k in range(4):
        put(4 + 8 * k, mixed[k][0] - mixed[k][1])
        put(NX - 4 - 8 * k, mixed[k][0] + mixed[k][1])


def separate(get, put):
    for b, value in enumerate(hartley8([get(8 * k) for k in range(8)])):
        put(b, 0, value)
    for first in range(1, 4):
        mixed = fourier8([(get(first + 8 * k), get(NX - first - 8 * k)) for k in range(8)], 1)
        for b in range(8):
            p, q = rotate(mixed[b], b * first, 1)
            put(b, first, p)
            put(b, 8 - first, q)
    mixed = fourier8([(get(4 + 8 * k), jnp.zeros_like(get(4))) for k in range(8)], 1)
    for b in range(8):
        p, q = rotate(mixed[b], b * 4, 1)
        put(b, 4, p + q)


def exchange_kernel(sticks, capacity, target, counts, facts, owned_far, source_far, mine, table_y, table_z,
                    kernel, out, owned, source, sem, slot, grid, turned, work, result, out_sem):
    stick, is_root, root_row = facts[0], facts[1], facts[2]
    length = capacity // PIECES
    unit = math.gcd(length, UNIT)
    span = math.gcd(length, SPAN)

    def fetch(block, piece):
        at = pl.ds(piece * length, length)
        here = block == stick
        from_mine = here & (is_root == 1)

        def bring(src, dst, which):
            pltpu.make_async_copy(src.at[at], dst.at[pl.ds(block * capacity + piece * length, length)],
                                  sem.at[which, block, piece]).start()

        pl.when(here)(lambda: bring(mine.at[block], owned, 0))
        pl.when(jnp.logical_not(here))(lambda: bring(owned_far.at[block], owned, 0))
        pl.when(from_mine)(lambda: bring(mine.at[root_row], source, 1))
        pl.when(jnp.logical_not(from_mine))(lambda: bring(source_far.at[block], source, 1))

    for block in range(sticks):
        for piece in range(PIECES):
            fetch(block, piece)

    offset = 0
    for block in range(sticks):
        for piece in range(PIECES):
            base = block * capacity + piece * length
            at = pl.ds(base, length)
            live = jnp.clip(counts[block] - piece * length, 0, length)
            start = offset + piece * length
            pltpu.make_async_copy(owned_far.at[0, pl.ds(0, length)], owned.at[at], sem.at[0, block, piece]).wait()
            pltpu.make_async_copy(source_far.at[0, pl.ds(0, length)], source.at[at], sem.at[1, block, piece]).wait()

            @pl.loop(0, pl.cdiv(live, span))
            def _(i):
                first = pl.multiple_of(base + i * span, span)
                value = source[pl.ds(first, span), :].astype(jnp.float32)
                slot[pl.ds(2 * first, span, stride=2), :] = owned[pl.ds(first, span), :].astype(jnp.float32) * value
                slot[pl.ds(2 * first + 1, span, stride=2), :] = value

            @pl.loop(0, pl.cdiv(live, unit))
            def _(j):
                for u in range(unit):
                    i = j * unit + u
                    grid[pl.ds(target[start + i], 2), :] = slot[pl.ds(2 * (base + i), 2), :]

        offset = offset + counts[block]

    plane = lambda x: pl.ds(x * NY, NY)
    within = lambda x, which: pl.ds(2 * NY * x + which, NY, stride=2)

    for b in range(8):
        value = []
        for a in range(0, 8, 2):
            both = jnp.concatenate([grid[within(8 * (a + i) + b, 0), :] for i in range(2)], axis=1)
            both = left(table_y[...], both)
            value += [both[:, :NZ], both[:, NZ:]]
        for k, part in enumerate(hartley8(value)):
            turned[plane(8 * b + k), :] = part

    def part_of(j):
        return lambda x: pl.ds(pl.multiple_of(x * NY + j * LINES, LINES), LINES)

    @pl.loop(0, NY // LINES)
    def _(j):
        at = part_of(j)
        combine(lambda b, k: turned[at(8 * b + k), :], lambda x, v: work.__setitem__((at(x), slice(None)), v))

    for i in range(NX * NY // ROWS):
        at = pl.ds(i * ROWS, ROWS)
        work[at, :] = along_z(along_z(work[at, :], table_z[...]) * kernel[at, :], table_z[...])

    @pl.loop(0, NY // LINES)
    def _(j):
        at = part_of(j)
        separate(lambda x: work[at(x), :], lambda b, k, v: turned.__setitem__((at(8 * b + k), slice(None)), v))

    sends = [pltpu.make_async_copy(result.at[:, b], out.at[:, b], out_sem.at[b]) for b in range(8)]
    for b in range(8):
        value = hartley8([turned[plane(8 * b + k), :] for k in range(8)])
        for a in range(0, 8, 2):
            both = left(table_y[...], jnp.concatenate(value[a:a + 2], axis=1))
            for i in range(2):
                x = 8 * (a + i) + b
                part = both[:, i * NZ:(i + 1) * NZ]
                result[a + i, b] = (part * grid[within(x, 1), :]).astype(jnp.bfloat16)
        sends[b].start()
    for copy in sends:
        copy.wait()


def exchange(stick_perm, stick_counts, facts, owned, source, mine):
    sticks, capacity, depth = owned.shape
    table_y, low_y = halves(hartley_table(NY))
    table_z, low_z = halves(hartley_table(NZ))
    left_y = jnp.asarray(np.concatenate([table_y, table_y, low_y], axis=1))
    right_z = np.concatenate(
        [np.concatenate([table_z, low_z], axis=1), np.concatenate([table_z, np.zeros_like(low_z)], axis=1)], axis=0)
    right_z = jnp.asarray(right_z)
    kernel = screened(signed_freq(NX), signed_freq(NY), signed_freq(NZ)) * (-1.0 / (NX * NY * NZ))
    kernel = jnp.asarray(kernel.reshape(NX * NY, NZ), jnp.float32)
    target = jnp.pad(stick_perm * 2, (0, UNIT), constant_values=2 * NX * NY)
    smem = pl.BlockSpec(memory_space=pltpu.SMEM)
    vmem = pl.BlockSpec(memory_space=pltpu.VMEM)
    anywhere = pl.BlockSpec(memory_space=pl.ANY)
    slots = sticks * capacity
    full = lambda n: pltpu.VMEM((n, NZ), jnp.float32)
    return pl.pallas_call(
        functools.partial(exchange_kernel, sticks, capacity),
        out_shape=jax.ShapeDtypeStruct((NX // 8, 8, NY, NZ), jnp.bfloat16),
        in_specs=[smem] * 3 + [anywhere] * 3 + [vmem] * 3,
        out_specs=anywhere,
        scratch_shapes=[pltpu.VMEM((slots, NZ), jnp.bfloat16), pltpu.VMEM((slots, NZ), jnp.bfloat16),
                        pltpu.SemaphoreType.DMA((2, sticks, PIECES)), full(2 * slots), full(2 * NX * NY + 8), full(NX * NY),
                        full(NX * NY), pltpu.VMEM((NX // 8, 8, NY, NZ), jnp.bfloat16), pltpu.SemaphoreType.DMA((8,))],
        compiler_params=pltpu.CompilerParams(vmem_limit_bytes=40 << 20),
    )(target, stick_counts, facts, owned, source, mine, left_y, right_z, kernel)


def local(orbital_sticks, stick_perm, stick_counts, source_ids):
    sticks = lax.axis_size("stick")
    bands = lax.axis_size("band")
    rows = orbital_sticks.shape[0]
    group = lax.div(source_ids[0], rows)
    row = lax.rem(source_ids[0], rows)
    lines = bands // (WIDE * CORES)
    fits = orbital_sticks.shape[1] % (16 * math.lcm(2 * EACH, PARTS)) == 0
    if sticks == 2 and lines * WIDE * CORES == bands and bands <= 16 and fits:
        branches = [functools.partial(spread, root, lines) for root in range(bands)]
        source, owned = lax.switch(group, branches, lax.rem(source_ids, rows), orbital_sticks)
    else:
        piece = lax.dynamic_index_in_dim(orbital_sticks, row, 0, keepdims=False)
        source, owned = spread_far(group, piece, orbital_sticks)
    is_root = (lax.axis_index("band") == group).astype(jnp.int32)
    facts = jnp.stack([lax.axis_index("stick"), is_root, row]).astype(jnp.int32)
    out = exchange(stick_perm, stick_counts, facts, owned, source, orbital_sticks)
    return out.reshape(1, NX, NY, NZ)


def solution(mesh):
    placed = (P("band", "stick", None), P(), P(), P())
    return jax.shard_map(
        local,
        mesh=mesh,
        in_specs=placed,
        out_specs=P(("band", "stick"), None, None, None),
        check_vma=False,
    )
```
